256 devices in a mesh: lon: 32 (over z, x_lo, core), mem: 8 (over y, x_hi).
Axes of the slice: x: 4 (x_hi: 2, x_lo: 2; x = x_hi * 2 + x_lo), y: 4, z: 8, core: 2. Of those that a mesh axis runs over, the one named last changes fastest.
Arguments:
- assimilated_snapshot: bfloat16 [8, 1440, 128], P(None, 'lon'), may hold values from -6 to 6
- stochastic_displacement: bfloat16 [8, 8, 1440, 128], P('mem', None, 'lon'), may hold values from -3 to 3
- outcome_cotangent_vector: bfloat16 [8, 8, 1440, 128], P('mem', None, 'lon'), may hold values from -6 to 6
- spatial_window_coefficients: bfloat16 [3, 1152, 128], replicated, may hold values from -0.1875 to 0.1875
- mixer_entry_projection: bfloat16 [3, 128, 512], replicated, may hold values from -0.5 to 0.5
- mixer_exit_projection: bfloat16 [3, 512, 128], replicated, may hold values from -0.25 to 0.25
- spacing_per_tier: int32 [3], replicated, may hold values from 1 to 144, as said below
Outputs:
- trajectory_outcomes: bfloat16 [8, 8, 1440, 128], P('mem', None, 'lon')
- starting_point_partials: bfloat16 [8, 8, 1440, 128], P('mem', None, 'lon')
- filter_weight_derivative: float32 [3, 1152, 128], P(None, 'mem')
The draws below stay inside these ranges and needn't reach their ends.
Inputs may be any that keep to these rules, and one draw needn't show every extreme that they name: `spacing_per_tier`: dilations count longitude columns; in every draw some layer has dilation 144.
All inputs are finite; a program needn't handle non-finite values.
Results may differ from the reference program's by a relative error of at most 0.028.
Values may be sent and summed in bfloat16 or wider, within the bound.
No kernel may reach another device: no remote copies, remote signals or barrier semaphores. Data moves between devices by JAX's collectives and lax.ppermute only.
A program may use at most 64 MiB of HBM per device.

```python
import math
import jax
import jax.numpy as jnp
from jax import lax

FEATURE_DEPTH = 128
HID = 512
MAXD = 144
PARALLEL_ROWS = 8
LAYERS = 3
MERIDIAN_COUNT = 1440
TRAJECTORY_COUNT = 8


def draw_spacing_per_tier(key, part):
    base = jax.random.fold_in(key, 7)
    first_key, second_key = jax.random.split(base)
    values = jax.random.randint(first_key, (LAYERS,), 1, MAXD + 1)
    chosen = jax.random.randint(second_key, (), 0, LAYERS)
    return jnp.where(jnp.arange(LAYERS) == chosen, MAXD, values).astype(jnp.int32)


def steps_of(stream_key, extent, cuts, smallest, top_value):
    gain = 1.0
    for position, parts in cuts:
        steps = jax.random.uniform(jax.random.fold_in(jax.random.fold_in(stream_key, 6), position), (parts,), jnp.float32, smallest / len(cuts), top_value / len(cuts))
        gain = gain * jnp.repeat(jnp.exp(steps), extent[position] // parts).reshape((-1,) + (1,) * (len(extent) - 1 - position))
    return gain


def gaussian(key, extent, scale, limit, cuts=(), kind=jnp.bfloat16):
    entries = scale * jax.random.normal(key, extent, jnp.float32)
    if cuts:
        entries = entries * steps_of(key, extent, cuts, -0.22, 0.18)
    return jnp.clip(entries, -limit, limit).astype(kind)


def setup_inputs(seed: int = 0) -> dict:
    seeds = jax.random.split(jax.random.key(seed), 8)
    return {
        "assimilated_snapshot": gaussian(seeds[0], (PARALLEL_ROWS, MERIDIAN_COUNT, FEATURE_DEPTH), 1.0, 6.0, ((1, 32),)),
        "stochastic_displacement": gaussian(seeds[1], (TRAJECTORY_COUNT, PARALLEL_ROWS, MERIDIAN_COUNT, FEATURE_DEPTH), 0.5, 3.0, ((0, 8), (2, 32))),
        "outcome_cotangent_vector": gaussian(seeds[2], (TRAJECTORY_COUNT, PARALLEL_ROWS, MERIDIAN_COUNT, FEATURE_DEPTH), 1.0, 6.0, ((0, 8), (2, 32))),
        "spatial_window_coefficients": gaussian(seeds[3], (LAYERS, 9 * FEATURE_DEPTH, FEATURE_DEPTH), (9 * FEATURE_DEPTH) ** -0.5, 0.1875),
        "mixer_entry_projection": gaussian(seeds[4], (LAYERS, FEATURE_DEPTH, HID), FEATURE_DEPTH ** -0.5, 0.5),
        "mixer_exit_projection": gaussian(seeds[5], (LAYERS, HID, FEATURE_DEPTH), HID ** -0.5, 0.25),
        "spacing_per_tier": draw_spacing_per_tier(jax.random.fold_in(seeds[7], 71), 0),
    }


def slope(values):
    sig = jax.nn.sigmoid(values)
    return sig * (1.0 + values * (1.0 - sig))

def tap_matrix(field, dilation):
    lat_rows = field.shape[0]
    padded = jnp.pad(field, ((1, 1), (0, 0), (0, 0)))
    pieces = []
    for row_off in range(3):
        rows = padded[row_off:row_off + lat_rows]
        for col_off in range(3):
            pieces.append(jnp.roll(rows, -(col_off - 1) * dilation, axis=1))
    return jnp.concatenate(pieces, axis=2).reshape(-1, 9 * field.shape[2])

def flipped_kernel(kernel, chans):
    return jnp.transpose(kernel.reshape(9, chans, chans)[::-1], (0, 2, 1)).reshape(9 * chans, chans)

def reference(assimilated_snapshot, stochastic_displacement, outcome_cotangent_vector, spatial_window_coefficients, mixer_entry_projection, mixer_exit_projection, spacing_per_tier):
    lat_rows, lon_cols, chans = assimilated_snapshot.shape

    def solitary_trajectory(pair):
        pert, cot = pair
        latent_activation = (assimilated_snapshot.astype(jnp.float32) + pert.astype(jnp.float32)).astype(jnp.bfloat16)
        saved = []
        for layer in range(LAYERS):
            taps = tap_matrix(latent_activation, spacing_per_tier[layer])
            pre_conv = jnp.dot(taps, spatial_window_coefficients[layer], preferred_element_type=jnp.float32)
            mixed = latent_activation.reshape(-1, chans).astype(jnp.float32) + jax.nn.silu(pre_conv)
            pre_mlp = jnp.dot(mixed.astype(jnp.bfloat16), mixer_entry_projection[layer], preferred_element_type=jnp.float32)
            act_mlp = jax.nn.silu(pre_mlp).astype(jnp.bfloat16)
            outflow = mixed + jnp.dot(act_mlp, mixer_exit_projection[layer], preferred_element_type=jnp.float32)
            latent_activation = outflow.astype(jnp.bfloat16).reshape(lat_rows, lon_cols, chans)
            saved.append((taps, pre_conv, pre_mlp))
        trajectory_outcomes = latent_activation
        chain_rule_traversal = cot
        partial_pieces = [None] * LAYERS
        for layer in reversed(range(LAYERS)):
            taps, pre_conv, pre_mlp = saved[layer]
            back_flat = chain_rule_traversal.reshape(-1, chans)
            grad_pre_mlp = (jnp.dot(back_flat, mixer_exit_projection[layer].T, preferred_element_type=jnp.float32) * slope(pre_mlp)).astype(jnp.bfloat16)
            grad_mixed = back_flat.astype(jnp.float32) + jnp.dot(grad_pre_mlp, mixer_entry_projection[layer].T, preferred_element_type=jnp.float32)
            grad_conv = (grad_mixed * slope(pre_conv)).astype(jnp.bfloat16)
            partial_pieces[layer] = jnp.dot(taps.T, grad_conv, preferred_element_type=jnp.float32)
            grad_taps = tap_matrix(grad_conv.reshape(lat_rows, lon_cols, chans), spacing_per_tier[layer])
            adjoint = jnp.dot(grad_taps, flipped_kernel(spatial_window_coefficients[layer], chans), preferred_element_type=jnp.float32)
            chain_rule_traversal = (grad_mixed + adjoint).astype(jnp.bfloat16).reshape(lat_rows, lon_cols, chans)
        return (trajectory_outcomes, chain_rule_traversal, jnp.stack(partial_pieces))
    trajectory_outcomes, starting_point_partials, partial_pieces = lax.map(solitary_trajectory, (stochastic_displacement, outcome_cotangent_vector))
    scale = 1.0 / math.sqrt(TRAJECTORY_COUNT * PARALLEL_ROWS * MERIDIAN_COUNT)
    filter_weight_derivative = lax.optimization_barrier(jnp.sum(partial_pieces, axis=0)) * scale
    return (trajectory_outcomes, starting_point_partials, filter_weight_derivative)
```

```python
import math

import jax
import jax.numpy as jnp
from jax import lax
from jax.sharding import Mesh
from jax.sharding import PartitionSpec as P

MAXD = 144
LAYERS = 3
PLANE = ("xl", "core")
LON = ("z",) + PLANE


def passed_along(block, axis, distance):
    devices = range(lax.axis_size(axis))
    route = [((i - distance) % len(devices), i) for i in devices]
    return lax.ppermute(block, axis, route)


def slope(values):
    sig = jax.nn.sigmoid(values)
    return sig * (1.0 + values * (1.0 - sig))


def neighbour_columns(field, dilation):
    ncols = field.shape[1]
    hops = (MAXD + ncols - 1) // ncols

    def within(near):
        width = min(ncols, MAXD - near * ncols)

        def fetch(field):
            lower = passed_along(field[:, ncols - width :], LON, near + 1)
            upper = passed_along(field[:, :width], LON, -near - 1)
            pad = ((0, 0), (ncols - width, 0), (0, 0)), ((0, 0), (0, ncols - width), (0, 0))
            near_lower = passed_along(field, LON, near) if near else field
            near_upper = passed_along(field, LON, -near) if near else field
            return (
                jnp.pad(lower, pad[0]),
                near_lower,
                near_upper,
                jnp.pad(upper, pad[1]),
            )

        return fetch

    near = (dilation - 1) // ncols
    rest = dilation - near * ncols
    far_lower, near_lower, near_upper, far_upper = lax.switch(
        near, [within(k) for k in range(hops)], field
    )
    lower = jnp.concatenate([far_lower, near_lower], axis=1)
    upper = jnp.concatenate([near_upper, far_upper], axis=1)
    return (
        lax.dynamic_slice_in_dim(lower, ncols - rest, ncols, 1),
        lax.dynamic_slice_in_dim(upper, rest, ncols, 1),
    )


def layer_taps(field, dilation):
    lat_rows, ncols, chans = field.shape
    lower, upper = neighbour_columns(field, dilation)
    shifted = [jnp.pad(f, ((1, 1), (0, 0), (0, 0))) for f in (lower, field, upper)]
    pieces = [f[off : off + lat_rows] for off in range(3) for f in shifted]
    return jnp.concatenate(pieces, axis=2).reshape(-1, 9 * chans)


def total_over_all(partials):
    members = lax.axis_size("mem")
    layers, rows, chans = partials.shape
    own = rows // members
    terms = partials.astype(jnp.bfloat16).reshape(layers, members, own, chans)
    terms = lax.all_to_all(jnp.swapaxes(terms, 0, 1), "mem", 0, 0)
    part = jnp.sum(terms.astype(jnp.float32), axis=0).reshape(layers * own, chans)
    quarter = layers * own // 4
    plane = lax.all_gather(part.astype(jnp.bfloat16).reshape(4, quarter, chans), PLANE)
    place = 2 * lax.axis_index("xl") + lax.axis_index("core")
    mine = jnp.sum(plane.astype(jnp.float32), axis=0)
    mine = lax.dynamic_index_in_dim(mine, place, 0, False)
    sent = mine.astype(jnp.bfloat16)
    depth = lax.axis_size("z")
    came = [sent] + [passed_along(sent, "z", hop) for hop in range(1, depth)]
    twice = jnp.stack(came[::-1] * 2)
    ordered = lax.dynamic_slice_in_dim(twice, depth - 1 - lax.axis_index("z"), depth, 0)
    total = jnp.sum(ordered.astype(jnp.float32), axis=0)
    full = lax.all_gather(total.astype(jnp.bfloat16), PLANE)
    return full.reshape(layers, own, chans).astype(jnp.float32)


def flipped_kernel(kernel, chans):
    return jnp.transpose(kernel.reshape(9, chans, chans)[::-1], (0, 2, 1)).reshape(9 * chans, chans)


def per_device(
    assimilated_snapshot,
    stochastic_displacement,
    outcome_cotangent_vector,
    spatial_window_coefficients,
    mixer_entry_projection,
    mixer_exit_projection,
    spacing_per_tier,
):
    lat_rows, ncols, chans = assimilated_snapshot.shape
    latent_activation = (
        assimilated_snapshot.astype(jnp.float32) + stochastic_displacement[0].astype(jnp.float32)
    ).astype(jnp.bfloat16)
    saved = []
    for layer in range(LAYERS):
        taps = layer_taps(latent_activation, spacing_per_tier[layer])
        pre_conv = jnp.dot(
            taps, spatial_window_coefficients[layer], preferred_element_type=jnp.float32
        )
        mixed = latent_activation.reshape(-1, chans).astype(jnp.float32) + jax.nn.silu(pre_conv)
        pre_mlp = jnp.dot(
            mixed.astype(jnp.bfloat16),
            mixer_entry_projection[layer],
            preferred_element_type=jnp.float32,
        )
        act_mlp = jax.nn.silu(pre_mlp).astype(jnp.bfloat16)
        outflow = mixed + jnp.dot(
            act_mlp, mixer_exit_projection[layer], preferred_element_type=jnp.float32
        )
        latent_activation = outflow.astype(jnp.bfloat16).reshape(lat_rows, ncols, chans)
        saved.append((taps, pre_conv, pre_mlp))
    chain_rule_traversal = outcome_cotangent_vector[0]
    partial_pieces = [None] * LAYERS
    for layer in reversed(range(LAYERS)):
        taps, pre_conv, pre_mlp = saved[layer]
        back_flat = chain_rule_traversal.reshape(-1, chans)
        grad_pre_mlp = (
            jnp.dot(back_flat, mixer_exit_projection[layer].T, preferred_element_type=jnp.float32)
            * slope(pre_mlp)
        ).astype(jnp.bfloat16)
        grad_mixed = back_flat.astype(jnp.float32) + jnp.dot(
            grad_pre_mlp, mixer_entry_projection[layer].T, preferred_element_type=jnp.float32
        )
        grad_conv = (grad_mixed * slope(pre_conv)).astype(jnp.bfloat16)
        partial_pieces[layer] = lax.dot_general(
            taps, grad_conv, (((0,), (0,)), ((), ())), preferred_element_type=jnp.float32
        )
        grad_taps = layer_taps(grad_conv.reshape(lat_rows, ncols, chans), spacing_per_tier[layer])
        adjoint = jnp.dot(
            grad_taps,
            flipped_kernel(spatial_window_coefficients[layer], chans),
            preferred_element_type=jnp.float32,
        )
        chain_rule_traversal = (
            (grad_mixed + adjoint).astype(jnp.bfloat16).reshape(lat_rows, ncols, chans)
        )
    stacked = jnp.stack(partial_pieces)
    share = total_over_all(stacked)
    member_count = lax.axis_size("mem") * stochastic_displacement.shape[0]
    scale = 1.0 / math.sqrt(member_count * lat_rows * ncols * lax.axis_size(LON))
    return (latent_activation[None], chain_rule_traversal[None], share * scale)


def solution(mesh):
    fine = Mesh(mesh.devices.reshape(-1, 2, 2, mesh.shape["mem"]), LON + ("mem",))
    placed = (
        P(None, LON, None),
        P("mem", None, LON, None),
        P("mem", None, LON, None),
        P(),
        P(),
        P(),
        P(),
    )
    return jax.shard_map(
        per_device,
        mesh=fine,
        in_specs=placed,
        out_specs=(P("mem", None, LON, None), P("mem", None, LON, None), P(None, "mem", None)),
        check_vma=False,
    )
```

```python
import functools
import math

import jax
import jax.numpy as jnp
from jax import lax
from jax.experimental import pallas as pl
from jax.experimental.pallas import tpu as pltpu
from jax.sharding import Mesh
from jax.sharding import PartitionSpec as P

MAXD = 144
LAYERS = 3
PLANE = ("xl", "core")
LON = ("z",) + PLANE
F32 = jnp.float32
BF16 = jnp.bfloat16


def passed_along(block, axis, distance):
    devices = range(lax.axis_size(axis))
    route = [((i - distance) % len(devices), i) for i in devices]
    return lax.ppermute(block, axis, route)


def slope(values):
    sig = jax.nn.sigmoid(values)
    return sig * (1.0 + values * (1.0 - sig))


def matmul(a, b, dims=((1,), (0,))):
    return lax.dot_general(a, b, (dims, ((), ())), preferred_element_type=F32)


def exchange(field, dilation, ncols):
    hops = (MAXD + ncols - 1) // ncols

    def within(near):
        def fetch(field):
            return (
                passed_along(field, LON, near + 1),
                passed_along(field, LON, near) if near else field,
                passed_along(field, LON, -near) if near else field,
                passed_along(field, LON, -near - 1),
            )

        return fetch

    near = (dilation - 1) // ncols
    return lax.switch(near, [within(k) for k in range(hops)], field)


class Sizes:
    def __init__(self, rows, ncols, chans, hidden):
        self.rows, self.ncols, self.chans, self.hidden = rows, ncols, chans, hidden
        self.pitch = (ncols + 15) // 16 * 16
        self.cells = rows * self.pitch


def fill_shifted(size, rest, parts, scratches):
    far_lower, near_lower, own, near_upper, far_upper = parts
    pitch, ncols = size.pitch, size.ncols
    shape = (pitch, 2 * pitch)
    col = lax.broadcasted_iota(jnp.int32, shape, 0)
    src = lax.broadcasted_iota(jnp.int32, shape, 1)
    live = (col < ncols) & (src < 2 * pitch)
    at = jnp.where(src < pitch, src, src - pitch + ncols)
    live = live & ((src < ncols) | ((src >= pitch) & (src < pitch + ncols)))
    picks = []
    for begin in (ncols - rest, rest):
        picks.append(jnp.where(live & (at == col + begin), 1.0, 0.0).astype(BF16))
    zero = jnp.zeros((pitch, size.chans), BF16)
    for scratch in scratches:
        scratch[pl.ds(0, pitch), :] = zero
        scratch[pl.ds(pitch + size.cells, pitch), :] = zero
    scratches[1][pl.ds(pitch, size.cells), :] = own
    for pick, first, second, scratch in (
        (picks[0], far_lower, near_lower, scratches[0]),
        (picks[1], near_upper, far_upper, scratches[2]),
    ):
        for row in range(size.rows):
            span = pl.ds(row * pitch, pitch)
            pair = jnp.concatenate([first[span, :], second[span, :]], axis=0)
            scratch[pl.ds(pitch + row * pitch, pitch), :] = matmul(pick, pair).astype(BF16)


def taps_of(size, scratches):
    pieces = []
    for off in range(3):
        for scratch in scratches:
            pieces.append(scratch[pl.ds(off * size.pitch, size.cells), :])
    return jnp.concatenate(pieces, axis=1)


def valid_cells(size):
    col = lax.broadcasted_iota(jnp.int32, (size.rows, size.pitch, 1), 1)
    return (col < size.ncols).reshape(size.cells, 1)


def padded_into(size, scratch, values):
    scratch[...] = jnp.zeros(scratch.shape, scratch.dtype)
    for row in range(size.rows):
        scratch[pl.ds(row * size.pitch, size.ncols), :] = values(row).astype(scratch.dtype)


def unpadded_into(size, out, values):
    for row in range(size.rows):
        out[row] = values[row * size.pitch : row * size.pitch + size.ncols, :].astype(out.dtype)


def forward_math(size, taps, own, kernel, entry, leave):
    pre_conv = matmul(taps, kernel)
    mixed = own.astype(F32) + pre_conv * jax.nn.sigmoid(pre_conv)
    narrow = mixed.astype(BF16)
    pre_mlp = matmul(narrow, entry)
    act = (pre_mlp * jax.nn.sigmoid(pre_mlp)).astype(BF16)
    return pre_conv, narrow, pre_mlp, mixed + matmul(act, leave)


def backward_math(size, back, pre_mlp, pre_conv, entry, leave):
    grad_pre = (matmul(back, leave, ((1,), (1,))) * slope(pre_mlp)).astype(BF16)
    grad_mixed = back.astype(F32) + matmul(grad_pre, entry, ((1,), (1,)))
    grad_conv = (grad_mixed * slope(pre_conv)).astype(BF16)
    return grad_mixed, grad_conv


def kernel_terms_into(size, out, taps, grad_conv):
    terms = matmul(grad_conv, taps, ((0,), (0,)))
    chans = size.chans
    for tap in range(9):
        out[pl.ds(tap * chans, chans), :] = terms[:, tap * chans : (tap + 1) * chans].T.astype(
            out.dtype
        )


def adjoint_math(size, taps, kernel_ref):
    chans = size.chans
    turned = jnp.concatenate(
        [kernel_ref[pl.ds((8 - tap) * chans, chans), :] for tap in range(9)], axis=1
    )
    return matmul(taps, turned, ((1,), (1,)))


def begin_body(size, a_ref, b_ref, out_ref):
    padded_into(
        size, out_ref, lambda row: a_ref[row].astype(F32) + b_ref[row].astype(F32)
    )


def forward_body(size, rest_ref, own, fl, nl, nu, fu, kernel, entry, leave, *rest):
    hidden, mixed_out, pre_conv_out, lower, upper, middle = rest
    shifted = (lower, middle, upper)
    fill_shifted(size, rest_ref[0], (fl, nl, own[...], nu, fu), shifted)
    pre_conv, narrow, _, total = forward_math(
        size, taps_of(size, shifted), own[...], kernel[...], entry[...], leave[...]
    )
    hidden[...] = jnp.where(valid_cells(size), total, 0.0).astype(BF16)
    mixed_out[...] = narrow
    pre_conv_out[...] = pre_conv


def turn_body(size, rest_ref, own, fl, nl, nu, fu, kernel, entry, leave, cot, *rest):
    outcome, grad_conv_out, grad_mixed_out, terms_out, lower, middle, upper, back = rest
    shifted = (lower, middle, upper)
    fill_shifted(size, rest_ref[0], (fl, nl, own[...], nu, fu), shifted)
    taps = taps_of(size, shifted)
    pre_conv, _, pre_mlp, total = forward_math(
        size, taps, own[...], kernel[...], entry[...], leave[...]
    )
    unpadded_into(size, outcome, total)
    padded_into(size, back, lambda row: cot[row])
    grad_mixed, grad_conv = backward_math(
        size, back[...], pre_mlp, pre_conv, entry[...], leave[...]
    )
    grad_conv_out[...] = grad_conv
    grad_mixed_out[...] = grad_mixed
    kernel_terms_into(size, terms_out, taps, grad_conv)


def backward_body(
    size, rest_ref, own, fl, nl, nu, fu, grad_mixed_in, kernel,
    hidden, mixed, pre_conv, x_lower, x_upper, entry, leave, *rest
):
    grad_conv_out, grad_mixed_out, terms_out, lower, middle, upper = rest
    shifted = (lower, middle, upper)
    fill_shifted(size, rest_ref[0], (fl, nl, own[...], nu, fu), shifted)
    total = grad_mixed_in[...] + adjoint_math(size, taps_of(size, shifted), kernel)
    back = jnp.where(valid_cells(size), total, 0.0).astype(BF16)
    pre_mlp = matmul(mixed[...], entry[...])
    grad_mixed, grad_conv = backward_math(
        size, back, pre_mlp, pre_conv[...], entry[...], leave[...]
    )
    grad_conv_out[...] = grad_conv
    grad_mixed_out[...] = grad_mixed
    middle[pl.ds(size.pitch, size.cells), :] = hidden[...]
    kernel_terms_into(size, terms_out, taps_of(size, (x_lower, middle, x_upper)), grad_conv)


def finish_body(size, rest_ref, own, fl, nl, nu, fu, grad_mixed_in, kernel, *rest):
    out, lower, middle, upper = rest
    shifted = (lower, middle, upper)
    fill_shifted(size, rest_ref[0], (fl, nl, own[...], nu, fu), shifted)
    total = grad_mixed_in[...] + adjoint_math(size, taps_of(size, shifted), kernel)
    unpadded_into(size, out, total)


def call(body, size, name, args, outs, scratches=(), scalars=0):
    vmem = pl.BlockSpec(memory_space=pltpu.VMEM)
    smem = pl.BlockSpec(memory_space=pltpu.SMEM)
    return pl.pallas_call(
        functools.partial(body, size),
        out_shape=outs,
        in_specs=[smem] * scalars + [vmem] * (len(args) - scalars),
        out_specs=[vmem] * len(outs),
        scratch_shapes=[pltpu.VMEM(shape, dtype) for shape, dtype in scratches],
        name=name,
    )(*args)


def total_over_all(partials):
    members = lax.axis_size("mem")
    layers = len(partials)
    rows, chans = partials[0].shape
    own = rows // members
    terms = jnp.stack([p.reshape(members, own, chans) for p in partials], axis=1)
    terms = lax.all_to_all(terms, "mem", 0, 0)
    part = jnp.sum(terms.astype(F32), axis=0).reshape(layers * own, chans)
    quarter = layers * own // 4
    plane = lax.all_gather(part.astype(BF16).reshape(4, quarter, chans), PLANE)
    place = 2 * lax.axis_index("xl") + lax.axis_index("core")
    mine = jnp.sum(plane.astype(F32), axis=0)
    mine = lax.dynamic_index_in_dim(mine, place, 0, False)
    sent = mine.astype(BF16)
    planes = range(lax.axis_size("z"))
    came = [sent.astype(F32)]
    for flip in planes[1:]:
        came.append(lax.ppermute(sent, "z", [(i ^ flip, i) for i in planes]).astype(F32))
    while len(came) > 1:
        came = [a + b for a, b in zip(came[::2], came[1::2])]
    full = lax.all_gather(came[0].astype(BF16), PLANE)
    return full.reshape(layers, own, chans).astype(F32)


def per_device(
    assimilated_snapshot,
    stochastic_displacement,
    outcome_cotangent_vector,
    spatial_window_coefficients,
    mixer_entry_projection,
    mixer_exit_projection,
    spacing_per_tier,
):
    rows, ncols, chans = assimilated_snapshot.shape
    hidden_units = mixer_entry_projection.shape[2]
    size = Sizes(rows, ncols, chans, hidden_units)
    conv = [spatial_window_coefficients[i] for i in range(LAYERS)]
    entry = [mixer_entry_projection[i] for i in range(LAYERS)]
    leave = [mixer_exit_projection[i] for i in range(LAYERS)]
    near = (spacing_per_tier - 1) // ncols
    rest = spacing_per_tier - near * ncols
    rest = [rest[i : i + 1] for i in range(LAYERS)]
    field = jax.ShapeDtypeStruct((size.cells, chans), BF16)
    wide = jax.ShapeDtypeStruct((size.cells, chans), F32)
    tall = (size.cells + 2 * size.pitch, chans)
    edge = jax.ShapeDtypeStruct(tall, BF16)
    block = jax.ShapeDtypeStruct((rows, ncols, chans), BF16)
    terms = jax.ShapeDtypeStruct((9 * chans, chans), BF16)
    scratch = (tall, BF16)

    def swapped(values, layer):
        fl, nl, nu, fu = exchange(values, spacing_per_tier[layer], ncols)
        return (rest[layer], values, fl, nl, nu, fu)

    (hidden,) = call(
        begin_body, size, "begin", (assimilated_snapshot, stochastic_displacement[0]), [field]
    )
    saved = []
    for layer in range(LAYERS - 1):
        args = swapped(hidden, layer) + (conv[layer], entry[layer], leave[layer])
        after, mixed, pre_conv, lower, upper = call(
            forward_body, size, f"fwd{layer}", args,
            [field, field, wide, edge, edge], [scratch], 1,
        )
        saved.append((hidden, mixed, pre_conv, lower, upper))
        hidden = after
    last = LAYERS - 1
    args = swapped(hidden, last) + (conv[last], entry[last], leave[last])
    outcome, grad_conv, grad_mixed, term = call(
        turn_body, size, "turn", args + (outcome_cotangent_vector[0],),
        [block, field, wide, terms], [scratch] * 3 + [((size.cells, chans), BF16)], 1,
    )
    partials = [term]
    for layer in reversed(range(LAYERS - 1)):
        args = swapped(grad_conv, layer + 1) + (grad_mixed, conv[layer + 1])
        args += saved[layer] + (entry[layer], leave[layer])
        grad_conv, grad_mixed, term = call(
            backward_body, size, f"bwd{layer}", args, [field, wide, terms], [scratch] * 3, 1
        )
        partials.insert(0, term)
    args = swapped(grad_conv, 0) + (grad_mixed, conv[0])
    (first,) = call(finish_body, size, "finish", args, [block], [scratch] * 3, 1)
    share = total_over_all(partials)
    member_count = lax.axis_size("mem") * stochastic_displacement.shape[0]
    scale = 1.0 / math.sqrt(member_count * rows * ncols * lax.axis_size(LON))
    return (outcome[None], first[None], share * scale)


def solution(mesh):
    fine = Mesh(mesh.devices.reshape(-1, 2, 2, mesh.shape["mem"]), LON + ("mem",))
    placed = (
        P(None, LON, None),
        P("mem", None, LON, None),
        P("mem", None, LON, None),
        P(),
        P(),
        P(),
        P(),
    )
    return jax.shard_map(
        per_device,
        mesh=fine,
        in_specs=placed,
        out_specs=(P("mem", None, LON, None), P("mem", None, LON, None), P(None, "mem", None)),
        check_vma=False,
    )
```

```python
import functools
import math

import jax
import jax.numpy as jnp
from jax import lax
from jax.experimental import pallas as pl
from jax.experimental.pallas import tpu as pltpu
from jax.sharding import Mesh
from jax.sharding import PartitionSpec as P

MAXD = 144
LAYERS = 3
PLANE = ("xl", "core")
LON = ("z",) + PLANE
F32 = jnp.float32
BF16 = jnp.bfloat16


def passed_along(block, axis, distance):
    devices = range(lax.axis_size(axis))
    route = [((i - distance) % len(devices), i) for i in devices]
    return lax.ppermute(block, axis, route)


def slope(values):
    sig = jax.nn.sigmoid(values)
    return sig * (1.0 + values * (1.0 - sig))


def matmul(a, b, dims=((1,), (0,))):
    return lax.dot_general(a, b, (dims, ((), ())), preferred_element_type=F32)


def exchange(field, near, ncols):
    hops = (MAXD + ncols - 1) // ncols

    def within(near):
        def fetch(field):
            return (
                passed_along(field, LON, near + 1),
                passed_along(field, LON, near) if near else field,
                passed_along(field, LON, -near) if near else field,
                passed_along(field, LON, -near - 1),
            )

        return fetch

    return lax.switch(near, [within(k) for k in range(hops)], field)


class Sizes:
    def __init__(self, rows, ncols, chans, hidden):
        self.rows, self.ncols, self.chans, self.hidden = rows, ncols, chans, hidden
        self.pitch = (ncols + 15) // 16 * 16
        self.cells = rows * self.pitch


def fill_shifted(size, rest, parts, scratches):
    far_lower, near_lower, own, near_upper, far_upper = parts
    pitch, ncols = size.pitch, size.ncols
    shape = (pitch, 2 * pitch)
    col = lax.broadcasted_iota(jnp.int32, shape, 0)
    src = lax.broadcasted_iota(jnp.int32, shape, 1)
    live = (col < ncols) & (src < 2 * pitch)
    at = jnp.where(src < pitch, src, src - pitch + ncols)
    live = live & ((src < ncols) | ((src >= pitch) & (src < pitch + ncols)))
    picks = []
    for begin in (ncols - rest, rest):
        picks.append(jnp.where(live & (at == col + begin), 1.0, 0.0).astype(BF16))
    zero = jnp.zeros((pitch, size.chans), BF16)
    for scratch in scratches:
        scratch[pl.ds(0, pitch), :] = zero
        scratch[pl.ds(pitch + size.cells, pitch), :] = zero
    scratches[1][pl.ds(pitch, size.cells), :] = own
    for pick, first, second, scratch in (
        (picks[0], far_lower, near_lower, scratches[0]),
        (picks[1], near_upper, far_upper, scratches[2]),
    ):
        for row in range(size.rows):
            span = pl.ds(row * pitch, pitch)
            pair = jnp.concatenate([first[span, :], second[span, :]], axis=0)
            scratch[pl.ds(pitch + row * pitch, pitch), :] = matmul(pick, pair).astype(BF16)


def taps_of(size, scratches):
    pieces = []
    for off in range(3):
        for scratch in scratches:
            pieces.append(scratch[pl.ds(off * size.pitch, size.cells), :])
    return jnp.concatenate(pieces, axis=1)


def valid_cells(size):
    col = lax.broadcasted_iota(jnp.int32, (size.rows, size.pitch, 1), 1)
    return (col < size.ncols).reshape(size.cells, 1)


def padded_into(size, scratch, values):
    scratch[...] = jnp.zeros(scratch.shape, scratch.dtype)
    for row in range(size.rows):
        scratch[pl.ds(row * size.pitch, size.ncols), :] = values(row).astype(scratch.dtype)


def unpadded_into(size, out, values):
    for row in range(size.rows):
        out[row] = values[row * size.pitch : row * size.pitch + size.ncols, :].astype(out.dtype)


def silu(values):
    return values * jax.nn.sigmoid(values)


def begin_body(size, a_ref, b_ref, field, *unwritten):
    padded_into(size, field, lambda row: a_ref[row].astype(F32) + b_ref[row].astype(F32))


def stage_body(
    size, stage_ref, spacing_ref, fl, nl, nu, fu, entry, leave, cot, conv, field_in, grad_in, *refs
):
    field, grad_out, hidden, mixed, pre_conv, lower, upper, terms, outcome, first = refs[8:18]
    left, middle, right, back, kernel, own, narrow, pre, before, after, found, block, sems = refs[18:]
    stage = stage_ref[0]
    forward = stage < LAYERS
    turn = stage == LAYERS - 1
    final = stage == 2 * LAYERS - 1
    layer = jnp.where(forward, stage, 2 * LAYERS - 1 - stage)
    at = jnp.where(forward, stage, jnp.maximum(2 * LAYERS - 2 - stage, 0))
    kept = jnp.minimum(at, LAYERS - 2)
    inner = pl.ds(size.pitch, size.cells)
    pairs = (
        (hidden, own.at[inner]), (mixed, narrow), (pre_conv, pre), (lower, before), (upper, after)
    )
    weights = pltpu.make_async_copy(conv.at[layer], kernel, sems.at[0])
    loads = [
        pltpu.make_async_copy(there.at[kept], here, sems.at[1 + i])
        for i, (there, here) in enumerate(pairs)
    ]
    saves = [
        pltpu.make_async_copy(here, there.at[kept], sems.at[1 + i])
        for i, (there, here) in enumerate(pairs)
    ]
    weights.start()

    @pl.when(~forward & ~final)
    def _():
        for copy in loads:
            copy.start()

    spacing = spacing_ref[layer]
    near = sum((spacing > hop * size.ncols).astype(jnp.int32) for hop in range(1, size.hops))
    shifted = (left, middle, right)
    fill_shifted(size, spacing - near * size.ncols, (fl, nl, field_in[...], nu, fu), shifted)
    weights.wait()

    @pl.when(forward)
    def _():
        mine = middle[inner, :]
        taps = taps_of(size, shifted)
        before[...] = left[...]
        after[...] = right[...]
        own[...] = middle[...]
        value = matmul(taps, kernel[...])
        total = mine.astype(F32) + silu(value)
        small = total.astype(BF16)
        pre[...] = value
        narrow[...] = small
        act = silu(matmul(small, entry[at])).astype(BF16)
        total = total + matmul(act, leave[at])

        @pl.when(~turn)
        def _():
            for copy in saves:
                copy.start()
            field[...] = jnp.where(valid_cells(size), total, 0.0).astype(BF16)
            for copy in saves:
                copy.wait()

        @pl.when(turn)
        def _():
            unpadded_into(size, block, total)
            copy = pltpu.make_async_copy(block, outcome, sems.at[6])
            copy.start()
            padded_into(size, back, lambda row: cot[row])
            copy.wait()

    @pl.when(~forward)
    def _():
        chans = size.chans
        turned = jnp.concatenate(
            [kernel[pl.ds((8 - tap) * chans, chans), :] for tap in range(9)], axis=1
        )
        total = grad_in[...] + matmul(taps_of(size, shifted), turned, ((1,), (1,)))
        back[...] = jnp.where(valid_cells(size), total, 0.0).astype(BF16)

        @pl.when(final)
        def _():
            unpadded_into(size, block, back)
            copy = pltpu.make_async_copy(block, first, sems.at[6])
            copy.start()
            copy.wait()

        @pl.when(~final)
        def _():
            own[pl.ds(0, size.pitch), :] = jnp.zeros((size.pitch, chans), BF16)
            own[pl.ds(size.pitch + size.cells, size.pitch), :] = jnp.zeros(
                (size.pitch, chans), BF16
            )
            for copy in loads:
                copy.wait()

    @pl.when((stage >= LAYERS - 1) & ~final)
    def _():
        came = back[...]
        pre_mlp = matmul(narrow[...], entry[at])
        grad_pre = (matmul(came, leave[at], ((1,), (1,))) * slope(pre_mlp)).astype(BF16)
        grad = came.astype(F32) + matmul(grad_pre, entry[at], ((1,), (1,)))
        grad_out[...] = grad
        grad_conv = (grad * slope(pre[...])).astype(BF16)
        field[...] = grad_conv
        taps = taps_of(size, (before, own, after))
        values = matmul(grad_conv, taps, ((0,), (0,)))
        chans = size.chans
        for tap in range(9):
            found[pl.ds(tap * chans, chans), :] = values[:, tap * chans : (tap + 1) * chans].T.astype(
                BF16
            )
        count = 9 * chans // size.members
        copies = []
        for member in range(size.members):
            to = pl.multiple_of(member * size.share + at * count, 16)
            copies.append(
                pltpu.make_async_copy(
                    found.at[pl.ds(member * count, count)],
                    terms.at[pl.ds(to, count)],
                    sems.at[7 + member],
                )
            )
        for copy in copies:
            copy.start()
        for copy in copies:
            copy.wait()


VMEM_SPEC = pl.BlockSpec(memory_space=pltpu.VMEM)
SMEM_SPEC = pl.BlockSpec(memory_space=pltpu.SMEM)
ANY_SPEC = pl.BlockSpec(memory_space=pl.ANY)


def total_over_all(size, terms):
    places = size.members * 4
    each = terms.shape[0] // places
    terms = lax.all_to_all(terms.reshape(places, each, size.chans), ("mem",) + PLANE, 0, 0)
    mine = jnp.sum(terms.astype(F32), axis=0).astype(BF16)
    planes = range(lax.axis_size("z"))
    came = [mine.astype(F32)]
    for flip in planes[1:]:
        came.append(lax.ppermute(mine, "z", [(i ^ flip, i) for i in planes]).astype(F32))
    while len(came) > 1:
        came = [a + b for a, b in zip(came[::2], came[1::2])]
    full = lax.all_gather(came[0].astype(BF16), PLANE).reshape(size.share, size.chans)
    own = 9 * size.chans // size.members
    return full[: LAYERS * own].reshape(LAYERS, own, size.chans).astype(F32)


def per_device(
    assimilated_snapshot,
    stochastic_displacement,
    outcome_cotangent_vector,
    spatial_window_coefficients,
    mixer_entry_projection,
    mixer_exit_projection,
    spacing_per_tier,
):
    rows, ncols, chans = assimilated_snapshot.shape
    size = Sizes(rows, ncols, chans, mixer_entry_projection.shape[2])
    size.hops = (MAXD + ncols - 1) // ncols
    size.members = lax.axis_size("mem")
    size.share = (LAYERS * 9 * chans // size.members + 63) // 64 * 64
    tall = (size.cells + 2 * size.pitch, chans)
    cells = (size.cells, chans)

    def array(*shape, dtype=BF16):
        return jax.ShapeDtypeStruct(shape, dtype)

    kinds = [
        array(*cells),
        array(*cells, dtype=F32),
        array(LAYERS - 1, *cells),
        array(LAYERS - 1, *cells),
        array(LAYERS - 1, *cells, dtype=F32),
        array(LAYERS - 1, *tall),
        array(LAYERS - 1, *tall),
        array(size.members * size.share, chans),
        array(rows, ncols, chans),
        array(rows, ncols, chans),
    ]
    held = len(kinds)
    state = pl.pallas_call(
        functools.partial(begin_body, size),
        out_shape=kinds,
        in_specs=[VMEM_SPEC] * 2,
        out_specs=[VMEM_SPEC] + [ANY_SPEC] * (held - 1),
        name="begin",
    )(assimilated_snapshot, stochastic_displacement[0])
    near = sum((spacing_per_tier > hop * ncols).astype(jnp.int32) for hop in range(1, size.hops))
    near = jnp.concatenate([near, near[::-1]])
    state_specs = [VMEM_SPEC] * 2 + [ANY_SPEC] * (held - 2)
    stage_call = pl.pallas_call(
        functools.partial(stage_body, size),
        out_shape=kinds,
        in_specs=[SMEM_SPEC] * 2 + [VMEM_SPEC] * 7 + [ANY_SPEC] + state_specs,
        out_specs=state_specs,
        scratch_shapes=[pltpu.VMEM(tall, BF16)] * 3
        + [
            pltpu.VMEM(cells, BF16),
            pltpu.VMEM((9 * chans, chans), BF16),
            pltpu.VMEM(tall, BF16),
            pltpu.VMEM(cells, BF16),
            pltpu.VMEM(cells, F32),
            pltpu.VMEM(tall, BF16),
            pltpu.VMEM(tall, BF16),
            pltpu.VMEM((9 * chans, chans), BF16),
            pltpu.VMEM((rows, ncols, chans), BF16),
            pltpu.SemaphoreType.DMA((7 + size.members,)),
        ],
        input_output_aliases={10 + i: i for i in range(held)},
        name="stage",
    )

    def step(stage, state):
        blocks = exchange(state[0], near[stage], ncols)
        return tuple(
            stage_call(
                stage.reshape(1),
                spacing_per_tier,
                *blocks,
                mixer_entry_projection,
                mixer_exit_projection,
                outcome_cotangent_vector[0],
                spatial_window_coefficients,
                *state,
            )
        )

    state = lax.fori_loop(0, 2 * LAYERS, step, tuple(state))
    share = total_over_all(size, state[7])
    member_count = size.members * stochastic_displacement.shape[0]
    scale = 1.0 / math.sqrt(member_count * rows * ncols * lax.axis_size(LON))
    return (state[8][None], state[9][None], share * scale)


def solution(mesh):
    fine = Mesh(mesh.devices.reshape(-1, 2, 2, mesh.shape["mem"]), LON + ("mem",))
    placed = (
        P(None, LON, None),
        P("mem", None, LON, None),
        P("mem", None, LON, None),
        P(),
        P(),
        P(),
        P(),
    )
    return jax.shard_map(
        per_device,
        mesh=fine,
        in_specs=placed,
        out_specs=(P("mem", None, LON, None), P("mem", None, LON, None), P(None, "mem", None)),
        check_vma=False,
    )
```

```python
import functools
import math

import jax
import jax.numpy as jnp
from jax import lax
from jax.experimental import pallas as pl
from jax.experimental.pallas import tpu as pltpu
from jax.sharding import Mesh
from jax.sharding import PartitionSpec as P

MAXD = 144
LAYERS = 3
PLANE = ("xl", "core")
LON = ("z",) + PLANE
F32 = jnp.float32
BF16 = jnp.bfloat16


def passed_along(block, axis, distance):
    devices = range(lax.axis_size(axis))
    route = [((i - distance) % len(devices), i) for i in devices]
    return lax.ppermute(block, axis, route)


def slope(values):
    sig = jax.nn.sigmoid(values)
    return sig * (1.0 + values * (1.0 - sig))


def matmul(a, b, dims=((1,), (0,))):
    return lax.dot_general(a, b, (dims, ((), ())), preferred_element_type=F32)


def exchange(field, near, ncols):
    hops = (MAXD + ncols - 1) // ncols

    def within(near):
        def fetch(field):
            return (
                passed_along(field, LON, near + 1),
                passed_along(field, LON, near) if near else field,
                passed_along(field, LON, -near) if near else field,
                passed_along(field, LON, -near - 1),
            )

        return fetch

    return lax.switch(near, [within(k) for k in range(hops)], field)


class Sizes:
    def __init__(self, rows, ncols, chans, hidden):
        self.rows, self.ncols, self.chans, self.hidden = rows, ncols, chans, hidden
        self.pitch = (ncols + 15) // 16 * 16
        self.cells = rows * self.pitch


def fill_shifted(size, rest, parts, scratches):
    far_lower, near_lower, own, near_upper, far_upper = parts
    pitch, ncols = size.pitch, size.ncols
    shape = (pitch, 2 * pitch)
    col = lax.broadcasted_iota(jnp.int32, shape, 0)
    src = lax.broadcasted_iota(jnp.int32, shape, 1)
    live = (col < ncols) & (src < 2 * pitch)
    at = jnp.where(src < pitch, src, src - pitch + ncols)
    live = live & ((src < ncols) | ((src >= pitch) & (src < pitch + ncols)))
    picks = []
    for begin in (ncols - rest, rest):
        picks.append(jnp.where(live & (at == col + begin), 1.0, 0.0).astype(BF16))
    zero = jnp.zeros((pitch, size.chans), BF16)
    for scratch in scratches:
        scratch[pl.ds(0, pitch), :] = zero
        scratch[pl.ds(pitch + size.cells, pitch), :] = zero
    scratches[1][pl.ds(pitch, size.cells), :] = own
    for pick, first, second, scratch in (
        (picks[0], far_lower, near_lower, scratches[0]),
        (picks[1], near_upper, far_upper, scratches[2]),
    ):
        for row in range(size.rows):
            span = pl.ds(row * pitch, pitch)
            pair = jnp.concatenate([first[span, :], second[span, :]], axis=0)
            scratch[pl.ds(pitch + row * pitch, pitch), :] = matmul(pick, pair).astype(BF16)


def taps_of(size, scratches):
    pieces = []
    for off in range(3):
        for scratch in scratches:
            pieces.append(scratch[pl.ds(off * size.pitch, size.cells), :])
    return jnp.concatenate(pieces, axis=1)


def valid_cells(size):
    col = lax.broadcasted_iota(jnp.int32, (size.rows, size.pitch, 1), 1)
    return (col < size.ncols).reshape(size.cells, 1)


def padded_into(size, scratch, values):
    scratch[...] = jnp.zeros(scratch.shape, scratch.dtype)
    for row in range(size.rows):
        scratch[pl.ds(row * size.pitch, size.ncols), :] = values(row).astype(scratch.dtype)


def unpadded_into(size, out, values):
    for row in range(size.rows):
        out[row] = values[row * size.pitch : row * size.pitch + size.ncols, :].astype(out.dtype)


def silu(values):
    return values * jax.nn.sigmoid(values)


def turned_into(size, scratch, out, values):
    scratch[...] = values.astype(F32).reshape(size.ncols * size.rows, size.chans)
    for row in range(size.rows):
        at = row * size.pitch
        out[pl.ds(at, size.ncols), :] = scratch[pl.ds(row, size.ncols, stride=size.rows), :].astype(
            out.dtype
        )


def terms_pieces(size, layer):
    count = 9 * size.chans // size.members
    pieces = []
    for member in range(size.members):
        row = layer * count
        while row < (layer + 1) * count:
            half = row // size.each
            end = min((half + 1) * size.each, (layer + 1) * count)
            to = (half * size.members + member) * size.each
            pieces.append((member * count + row - layer * count, to + row % size.each, end - row))
            row = end
    return pieces


def begin_body(size, a_ref, b_ref, *refs):
    field, scratch = refs[0], refs[-1]
    field[...] = jnp.zeros(field.shape, field.dtype)
    turned_into(size, scratch, field, a_ref[...].astype(F32) + b_ref[...].astype(F32))


def stage_body(
    size, stage_ref, spacing_ref, fl, nl, nu, fu, entry, leave, cot, conv, field_in, grad_in, *refs
):
    field, grad_out, hidden, mixed, pre_conv, lower, upper, terms, outcome, first = refs[8:18]
    left, middle, right, back, kernel, own, narrow, pre, before, after, found, block, wide, sems = refs[18:]
    stage = stage_ref[0]
    forward = stage < LAYERS
    turn = stage == LAYERS - 1
    final = stage == 2 * LAYERS - 1
    layer = jnp.where(forward, stage, 2 * LAYERS - 1 - stage)
    at = jnp.where(forward, stage, jnp.maximum(2 * LAYERS - 2 - stage, 0))
    kept = jnp.minimum(at, LAYERS - 2)
    inner = pl.ds(size.pitch, size.cells)
    pairs = (
        (hidden, own.at[inner]), (mixed, narrow), (pre_conv, pre), (lower, before), (upper, after)
    )
    weights = pltpu.make_async_copy(conv.at[layer], kernel, sems.at[0])
    loads = [
        pltpu.make_async_copy(there.at[kept], here, sems.at[1 + i])
        for i, (there, here) in enumerate(pairs)
    ]
    saves = [
        pltpu.make_async_copy(here, there.at[kept], sems.at[1 + i])
        for i, (there, here) in enumerate(pairs)
    ]
    weights.start()

    @pl.when(~forward & ~final)
    def _():
        for copy in loads:
            copy.start()

    spacing = spacing_ref[layer]
    near = sum((spacing > hop * size.ncols).astype(jnp.int32) for hop in range(1, size.hops))
    shifted = (left, middle, right)
    fill_shifted(size, spacing - near * size.ncols, (fl, nl, field_in[...], nu, fu), shifted)
    weights.wait()

    @pl.when(forward)
    def _():
        mine = middle[inner, :]
        taps = taps_of(size, shifted)
        before[...] = left[...]
        after[...] = right[...]
        own[...] = middle[...]
        value = matmul(taps, kernel[...])
        total = mine.astype(F32) + silu(value)
        small = total.astype(BF16)
        pre[...] = value
        narrow[...] = small
        act = silu(matmul(small, entry[at])).astype(BF16)
        total = total + matmul(act, leave[at])

        @pl.when(~turn)
        def _():
            for copy in saves:
                copy.start()
            field[...] = jnp.where(valid_cells(size), total, 0.0).astype(BF16)
            for copy in saves:
                copy.wait()

        @pl.when(turn)
        def _():
            unpadded_into(size, block, total)
            copy = pltpu.make_async_copy(block, outcome, sems.at[6])
            copy.start()
            back[...] = jnp.zeros(back.shape, back.dtype)
            turned_into(size, wide, back, cot[...])
            copy.wait()

    @pl.when(~forward)
    def _():
        chans = size.chans
        turned = jnp.concatenate(
            [kernel[pl.ds((8 - tap) * chans, chans), :] for tap in range(9)], axis=1
        )
        total = grad_in[...] + matmul(taps_of(size, shifted), turned, ((1,), (1,)))
        back[...] = jnp.where(valid_cells(size), total, 0.0).astype(BF16)

        @pl.when(final)
        def _():
            unpadded_into(size, block, back)
            copy = pltpu.make_async_copy(block, first, sems.at[6])
            copy.start()
            copy.wait()

        @pl.when(~final)
        def _():
            own[pl.ds(0, size.pitch), :] = jnp.zeros((size.pitch, chans), BF16)
            own[pl.ds(size.pitch + size.cells, size.pitch), :] = jnp.zeros(
                (size.pitch, chans), BF16
            )
            for copy in loads:
                copy.wait()

    @pl.when((stage >= LAYERS - 1) & ~final)
    def _():
        came = back[...]
        pre_mlp = matmul(narrow[...], entry[at])
        grad_pre = (matmul(came, leave[at], ((1,), (1,))) * slope(pre_mlp)).astype(BF16)
        grad = came.astype(F32) + matmul(grad_pre, entry[at], ((1,), (1,)))
        grad_out[...] = grad
        grad_conv = (grad * slope(pre[...])).astype(BF16)
        field[...] = grad_conv
        taps = taps_of(size, (before, own, after))
        values = matmul(grad_conv, taps, ((0,), (0,)))
        chans = size.chans
        for tap in range(9):
            found[pl.ds(tap * chans, chans), :] = values[:, tap * chans : (tap + 1) * chans].T.astype(
                BF16
            )
        for index in range(LAYERS):

            @pl.when(at == index)
            def _(index=index):
                copies = []
                for begin, to, count in terms_pieces(size, index):
                    copies.append(
                        pltpu.make_async_copy(
                            found.at[pl.ds(begin, count)],
                            terms.at[pl.ds(to, count)],
                            sems.at[7 + len(copies)],
                        )
                    )
                for copy in copies:
                    copy.start()
                for copy in copies:
                    copy.wait()


VMEM_SPEC = pl.BlockSpec(memory_space=pltpu.VMEM)
SMEM_SPEC = pl.BlockSpec(memory_space=pltpu.SMEM)
ANY_SPEC = pl.BlockSpec(memory_space=pl.ANY)


def total_over_all(size, terms):
    terms = terms.reshape(2, size.members * size.each, size.chans)
    terms = jnp.sum(lax.all_to_all(terms, "core", 0, 0).astype(F32), axis=0).astype(BF16)
    terms = terms.reshape(size.members, size.each, size.chans)
    total = jnp.sum(lax.all_to_all(terms, "mem", 0, 0).astype(F32), axis=0).astype(BF16)
    depth = lax.axis_size("z")
    swaps = [("xl", [1, 0])]
    swaps += [("z", [i ^ 1 for i in range(depth)]), ("z", [i ^ 2 for i in range(depth)])]
    swaps += [("z", [depth - 1 - i for i in range(depth)])]
    for axis, partner in swaps:
        other = lax.ppermute(total, axis, list(enumerate(partner)))
        total = (total.astype(F32) + other.astype(F32)).astype(BF16)
    full = lax.all_gather(total, "core").reshape(2 * size.each, size.chans)
    own = 9 * size.chans // size.members
    return full[: LAYERS * own].reshape(LAYERS, own, size.chans).astype(F32)


def per_device(
    assimilated_snapshot,
    stochastic_displacement,
    outcome_cotangent_vector,
    spatial_window_coefficients,
    mixer_entry_projection,
    mixer_exit_projection,
    spacing_per_tier,
):
    rows, ncols, chans = assimilated_snapshot.shape
    size = Sizes(rows, ncols, chans, mixer_entry_projection.shape[2])
    size.hops = (MAXD + ncols - 1) // ncols
    size.members = lax.axis_size("mem")
    size.each = (LAYERS * 9 * chans // size.members + 31) // 32 * 16
    size.pieces = max(len(terms_pieces(size, layer)) for layer in range(LAYERS))
    tall = (size.cells + 2 * size.pitch, chans)
    cells = (size.cells, chans)

    def columns_first(values):
        return jnp.swapaxes(values, 0, 1)

    def array(*shape, dtype=BF16):
        return jax.ShapeDtypeStruct(shape, dtype)

    kinds = [
        array(*cells),
        array(*cells, dtype=F32),
        array(LAYERS - 1, *cells),
        array(LAYERS - 1, *cells),
        array(LAYERS - 1, *cells, dtype=F32),
        array(LAYERS - 1, *tall),
        array(LAYERS - 1, *tall),
        array(2 * size.members * size.each, chans),
        array(rows, ncols, chans),
        array(rows, ncols, chans),
    ]
    held = len(kinds)
    state = pl.pallas_call(
        functools.partial(begin_body, size),
        out_shape=kinds,
        in_specs=[VMEM_SPEC] * 2,
        out_specs=[VMEM_SPEC] + [ANY_SPEC] * (held - 1),
        scratch_shapes=[pltpu.VMEM((rows * ncols, chans), F32)],
        name="begin",
    )(columns_first(assimilated_snapshot), columns_first(stochastic_displacement[0]))
    near = [
        sum((spacing_per_tier[i] > hop * ncols).astype(jnp.int32) for hop in range(1, size.hops))
        for i in range(LAYERS)
    ]
    code = sum(n << (4 * i) for i, n in enumerate(near + near[::-1]))
    state_specs = [VMEM_SPEC] * 2 + [ANY_SPEC] * (held - 2)
    stage_call = pl.pallas_call(
        functools.partial(stage_body, size),
        out_shape=kinds,
        in_specs=[SMEM_SPEC] * 2 + [VMEM_SPEC] * 7 + [ANY_SPEC] + state_specs,
        out_specs=state_specs,
        scratch_shapes=[pltpu.VMEM(tall, BF16)] * 3
        + [
            pltpu.VMEM(cells, BF16),
            pltpu.VMEM((9 * chans, chans), BF16),
            pltpu.VMEM(tall, BF16),
            pltpu.VMEM(cells, BF16),
            pltpu.VMEM(cells, F32),
            pltpu.VMEM(tall, BF16),
            pltpu.VMEM(tall, BF16),
            pltpu.VMEM((9 * chans, chans), BF16),
            pltpu.VMEM((rows, ncols, chans), BF16),
            pltpu.VMEM((rows * ncols, chans), F32),
            pltpu.SemaphoreType.DMA((7 + size.pieces,)),
        ],
        input_output_aliases={10 + i: i for i in range(held)},
        name="stage",
    )

    def step(stage, state):
        *state, code = state
        blocks = exchange(state[0], code & 15, ncols)
        return (
            *stage_call(
                stage.reshape(1),
                spacing_per_tier,
                *blocks,
                mixer_entry_projection,
                mixer_exit_projection,
                columns_first(outcome_cotangent_vector[0]),
                spatial_window_coefficients,
                *state,
            ),
            code >> 4,
        )

    state = lax.fori_loop(0, 2 * LAYERS, step, (*state, code))
    share = total_over_all(size, state[7])
    member_count = size.members * stochastic_displacement.shape[0]
    scale = 1.0 / math.sqrt(member_count * rows * ncols * lax.axis_size(LON))
    return (state[8][None], state[9][None], share * scale)


def solution(mesh):
    fine = Mesh(mesh.devices.reshape(-1, 2, 2, mesh.shape["mem"]), LON + ("mem",))
    placed = (
        P(None, LON, None),
        P("mem", None, LON, None),
        P("mem", None, LON, None),
        P(),
        P(),
        P(),
        P(),
    )
    return jax.shard_map(
        per_device,
        mesh=fine,
        in_specs=placed,
        out_specs=(P("mem", None, LON, None), P("mem", None, LON, None), P(None, "mem", None)),
        check_vma=False,
    )
```

```python
import functools
import math

import jax
import jax.numpy as jnp
from jax import lax
from jax.experimental import pallas as pl
from jax.experimental.pallas import tpu as pltpu
from jax.sharding import Mesh
from jax.sharding import PartitionSpec as P

MAXD = 144
LAYERS = 3
PLANE = ("xl", "core")
LON = ("z",) + PLANE
F32 = jnp.float32
BF16 = jnp.bfloat16


def passed_along(block, axis, distance):
    devices = range(lax.axis_size(axis))
    route = [((i - distance) % len(devices), i) for i in devices]
    return lax.ppermute(block, axis, route)


def slope(values):
    sig = jax.nn.sigmoid(values)
    return sig * (1.0 + values * (1.0 - sig))


def matmul(a, b, dims=((1,), (0,))):
    return lax.dot_general(a, b, (dims, ((), ())), preferred_element_type=F32)


def exchange(field, near, ncols):
    hops = (MAXD + ncols - 1) // ncols

    def within(near):
        def fetch(field):
            return (
                passed_along(field, LON, near + 1),
                passed_along(field, LON, near) if near else field,
                passed_along(field, LON, -near) if near else field,
                passed_along(field, LON, -near - 1),
            )

        return fetch

    return lax.switch(near, [within(k) for k in range(hops)], field)


class Sizes:
    def __init__(self, rows, ncols, chans, hidden):
        self.rows, self.ncols, self.chans, self.hidden = rows, ncols, chans, hidden
        self.pitch = (ncols + 15) // 16 * 16
        self.cells = rows * self.pitch


def fill_shifted(size, rest, parts, scratches):
    far_lower, near_lower, own, near_upper, far_upper = parts
    pitch, ncols = size.pitch, size.ncols
    shape = (pitch, 2 * pitch)
    col = lax.broadcasted_iota(jnp.int32, shape, 0)
    src = lax.broadcasted_iota(jnp.int32, shape, 1)
    live = (col < ncols) & (src < 2 * pitch)
    at = jnp.where(src < pitch, src, src - pitch + ncols)
    live = live & ((src < ncols) | ((src >= pitch) & (src < pitch + ncols)))
    picks = []
    for begin in (ncols - rest, rest):
        picks.append(jnp.where(live & (at == col + begin), 1.0, 0.0).astype(BF16))
    zero = jnp.zeros((pitch, size.chans), BF16)
    for scratch in scratches:
        scratch[pl.ds(0, pitch), :] = zero
        scratch[pl.ds(pitch + size.cells, pitch), :] = zero
    scratches[1][pl.ds(pitch, size.cells), :] = own
    for pick, first, second, scratch in (
        (picks[0], far_lower, near_lower, scratches[0]),
        (picks[1], near_upper, far_upper, scratches[2]),
    ):
        for row in range(size.rows):
            span = pl.ds(row * pitch, pitch)
            pair = jnp.concatenate([first[span, :], second[span, :]], axis=0)
            scratch[pl.ds(pitch + row * pitch, pitch), :] = matmul(pick, pair).astype(BF16)


def taps_of(size, scratches):
    pieces = []
    for off in range(3):
        for scratch in scratches:
            pieces.append(scratch[pl.ds(off * size.pitch, size.cells), :])
    return jnp.concatenate(pieces, axis=1)


def valid_cells(size):
    col = lax.broadcasted_iota(jnp.int32, (size.rows, size.pitch, 1), 1)
    return (col < size.ncols).reshape(size.cells, 1)


def padded_into(size, scratch, values):
    scratch[...] = jnp.zeros(scratch.shape, scratch.dtype)
    for row in range(size.rows):
        scratch[pl.ds(row * size.pitch, size.ncols), :] = values(row).astype(scratch.dtype)


def unpadded_into(size, out, values):
    for row in range(size.rows):
        out[row] = values[row * size.pitch : row * size.pitch + size.ncols, :].astype(out.dtype)


def silu(values):
    return values * jax.nn.sigmoid(values)


def turned_into(size, scratch, out, values):
    scratch[...] = values.astype(F32).reshape(size.ncols * size.rows, size.chans)
    for row in range(size.rows):
        at = row * size.pitch
        out[pl.ds(at, size.ncols), :] = scratch[pl.ds(row, size.ncols, stride=size.rows), :].astype(
            out.dtype
        )


def terms_pieces(size, layer):
    count = 9 * size.chans // size.members
    pieces = []
    for member in range(size.members):
        row = layer * count
        while row < (layer + 1) * count:
            half = row // size.each
            end = min((half + 1) * size.each, (layer + 1) * count)
            to = (half * size.members + member) * size.each
            pieces.append((member * count + row - layer * count, to + row % size.each, end - row))
            row = end
    return pieces


def begin_body(size, a_ref, b_ref, *refs):
    field, scratch = refs[0], refs[-1]
    field[...] = jnp.zeros(field.shape, field.dtype)
    turned_into(size, scratch, field, a_ref[...].astype(F32) + b_ref[...].astype(F32))


def stage_body(
    size, stage_ref, spacing_ref, cot, fl, nl, nu, fu, entries, leaves, conv, field_in, grad_in, *refs
):
    field, grad_out, hidden, mixed, pre_conv, lower, upper, terms, outcome, first = refs[8:18]
    left, middle, right, back, kernel, own, narrow, pre, before, after, found, block = refs[18:30]
    wide, entry, leave, came_in, sems, more = refs[30:]
    stage = stage_ref[0]
    forward = stage < LAYERS
    turn = stage == LAYERS - 1
    final = stage == 2 * LAYERS - 1
    layer = jnp.where(forward, stage, 2 * LAYERS - 1 - stage)
    at = jnp.where(forward, stage, jnp.maximum(2 * LAYERS - 2 - stage, 0))
    inner = pl.ds(size.pitch, size.cells)
    blocks = [
        pltpu.make_async_copy(there, came_in.at[i], more.at[i])
        for i, there in enumerate((fl, nl, nu, fu))
    ]
    weights = [
        pltpu.make_async_copy(conv.at[layer], kernel, sems.at[0]),
        pltpu.make_async_copy(entries.at[at], entry, more.at[4]),
        pltpu.make_async_copy(leaves.at[at], leave, more.at[5]),
    ]
    kept = (hidden, mixed, pre_conv, lower, upper)
    loads = [
        pltpu.make_async_copy(there.at[at], here, sems.at[1 + i])
        for i, (there, here) in enumerate(zip(kept, (own.at[inner], narrow, pre, before, after)))
    ]
    saves = [
        pltpu.make_async_copy(here, there.at[at], sems.at[1 + i])
        for i, (there, here) in enumerate(zip(kept, (middle.at[inner], narrow, pre, left, right)))
    ]
    for copy in blocks + weights:
        copy.start()

    @pl.when(~forward & ~final)
    def _():
        for copy in loads:
            copy.start()

    spacing = spacing_ref[layer]
    near = sum((spacing > hop * size.ncols).astype(jnp.int32) for hop in range(1, size.hops))
    shifted = (left, middle, right)
    for copy in blocks:
        copy.wait()
    parts = (came_in.at[0], came_in.at[1], field_in[...], came_in.at[2], came_in.at[3])
    fill_shifted(size, spacing - near * size.ncols, parts, shifted)
    for copy in weights:
        copy.wait()

    @pl.when(forward)
    def _():
        for copy in (saves[0], saves[3], saves[4]):
            copy.start()
        mine = middle[inner, :]
        taps = taps_of(size, shifted)
        value = matmul(taps, kernel[...])
        total = mine.astype(F32) + silu(value)
        small = total.astype(BF16)
        pre[...] = value
        narrow[...] = small
        saves[1].start()
        saves[2].start()
        act = silu(matmul(small, entry[...])).astype(BF16)
        total = total + matmul(act, leave[...])

        @pl.when(~turn)
        def _():
            field[...] = jnp.where(valid_cells(size), total, 0.0).astype(BF16)

        @pl.when(turn)
        def _():
            unpadded_into(size, block, total)
            copy = pltpu.make_async_copy(block, outcome, sems.at[6])
            copy.start()
            back[...] = jnp.zeros(back.shape, back.dtype)
            turned_into(size, wide, back, cot[...])
            before[...] = left[...]
            after[...] = right[...]
            own[...] = middle[...]
            copy.wait()

        for copy in saves:
            copy.wait()

    @pl.when(~forward)
    def _():
        chans = size.chans
        turned = jnp.concatenate(
            [kernel[pl.ds((8 - tap) * chans, chans), :] for tap in range(9)], axis=1
        )
        total = grad_in[...] + matmul(taps_of(size, shifted), turned, ((1,), (1,)))
        back[...] = jnp.where(valid_cells(size), total, 0.0).astype(BF16)

        @pl.when(final)
        def _():
            unpadded_into(size, block, back)
            copy = pltpu.make_async_copy(block, first, sems.at[6])
            copy.start()
            copy.wait()

        @pl.when(~final)
        def _():
            own[pl.ds(0, size.pitch), :] = jnp.zeros((size.pitch, chans), BF16)
            own[pl.ds(size.pitch + size.cells, size.pitch), :] = jnp.zeros(
                (size.pitch, chans), BF16
            )
            for copy in loads:
                copy.wait()

    @pl.when((stage >= LAYERS - 1) & ~final)
    def _():
        came = back[...]
        pre_mlp = matmul(narrow[...], entry[...])
        grad_pre = (matmul(came, leave[...], ((1,), (1,))) * slope(pre_mlp)).astype(BF16)
        grad = came.astype(F32) + matmul(grad_pre, entry[...], ((1,), (1,)))
        grad_out[...] = grad
        grad_conv = (grad * slope(pre[...])).astype(BF16)
        field[...] = grad_conv
        taps = taps_of(size, (before, own, after))
        values = matmul(grad_conv, taps, ((0,), (0,)))
        chans = size.chans
        for tap in range(9):
            found[pl.ds(tap * chans, chans), :] = values[:, tap * chans : (tap + 1) * chans].T.astype(
                BF16
            )
        for index in range(LAYERS):

            @pl.when(at == index)
            def _(index=index):
                copies = []
                for begin, to, count in terms_pieces(size, index):
                    copies.append(
                        pltpu.make_async_copy(
                            found.at[pl.ds(begin, count)],
                            terms.at[pl.ds(to, count)],
                            sems.at[7 + len(copies)],
                        )
                    )
                for copy in copies:
                    copy.start()
                for copy in copies:
                    copy.wait()


VMEM_SPEC = pl.BlockSpec(memory_space=pltpu.VMEM)
SMEM_SPEC = pl.BlockSpec(memory_space=pltpu.SMEM)
ANY_SPEC = pl.BlockSpec(memory_space=pl.ANY)
HBM_SPEC = pl.BlockSpec(memory_space=pltpu.HBM)


def total_over_all(size, terms):
    terms = terms.reshape(2, size.members * size.each, size.chans)
    terms = jnp.sum(lax.all_to_all(terms, "core", 0, 0).astype(F32), axis=0).astype(BF16)
    terms = terms.reshape(size.members, size.each, size.chans)
    total = jnp.sum(lax.all_to_all(terms, "mem", 0, 0).astype(F32), axis=0).astype(BF16)
    depth = lax.axis_size("z")
    swaps = [("xl", [1, 0])]
    swaps += [("z", [i ^ 1 for i in range(depth)]), ("z", [i ^ 2 for i in range(depth)])]
    swaps += [("z", [depth - 1 - i for i in range(depth)])]
    for axis, partner in swaps:
        other = lax.ppermute(total, axis, list(enumerate(partner)))
        total = (total.astype(F32) + other.astype(F32)).astype(BF16)
    full = lax.all_gather(total, "core").reshape(2 * size.each, size.chans)
    own = 9 * size.chans // size.members
    return full[: LAYERS * own].reshape(LAYERS, own, size.chans).astype(F32)


def per_device(
    assimilated_snapshot,
    stochastic_displacement,
    outcome_cotangent_vector,
    spatial_window_coefficients,
    mixer_entry_projection,
    mixer_exit_projection,
    spacing_per_tier,
):
    rows, ncols, chans = assimilated_snapshot.shape
    size = Sizes(rows, ncols, chans, mixer_entry_projection.shape[2])
    size.hops = (MAXD + ncols - 1) // ncols
    size.members = lax.axis_size("mem")
    size.each = (LAYERS * 9 * chans // size.members + 31) // 32 * 16
    size.pieces = max(len(terms_pieces(size, layer)) for layer in range(LAYERS))
    tall = (size.cells + 2 * size.pitch, chans)
    cells = (size.cells, chans)

    def columns_first(values):
        return jnp.swapaxes(values, 0, 1)

    def array(*shape, dtype=BF16):
        return jax.ShapeDtypeStruct(shape, dtype)

    kinds = [
        array(*cells),
        array(*cells, dtype=F32),
        array(LAYERS, *cells),
        array(LAYERS, *cells),
        array(LAYERS, *cells, dtype=F32),
        array(LAYERS, *tall),
        array(LAYERS, *tall),
        array(2 * size.members * size.each, chans),
        array(rows, ncols, chans),
        array(rows, ncols, chans),
    ]
    held = len(kinds)
    state = pl.pallas_call(
        functools.partial(begin_body, size),
        out_shape=kinds,
        in_specs=[VMEM_SPEC] * 2,
        out_specs=[VMEM_SPEC, ANY_SPEC] + [HBM_SPEC] * 5 + [ANY_SPEC] * 3,
        scratch_shapes=[pltpu.VMEM((rows * ncols, chans), F32)],
        name="begin",
    )(columns_first(assimilated_snapshot), columns_first(stochastic_displacement[0]))
    near = sum((spacing_per_tier > hop * ncols).astype(jnp.int32) for hop in range(1, size.hops))
    order = jnp.arange(LAYERS)
    code = jnp.sum(near * ((1 << (4 * order)) + (1 << (4 * (2 * LAYERS - 1 - order)))))
    state_specs = [VMEM_SPEC] * 2 + [HBM_SPEC] * 5 + [ANY_SPEC] * 3
    stage_call = pl.pallas_call(
        functools.partial(stage_body, size),
        out_shape=kinds,
        in_specs=[SMEM_SPEC] * 2 + [VMEM_SPEC] + [HBM_SPEC] * 7 + state_specs,
        out_specs=state_specs,
        scratch_shapes=[pltpu.VMEM(tall, BF16)] * 3
        + [
            pltpu.VMEM(cells, BF16),
            pltpu.VMEM((9 * chans, chans), BF16),
            pltpu.VMEM(tall, BF16),
            pltpu.VMEM(cells, BF16),
            pltpu.VMEM(cells, F32),
            pltpu.VMEM(tall, BF16),
            pltpu.VMEM(tall, BF16),
            pltpu.VMEM((9 * chans, chans), BF16),
            pltpu.VMEM((rows, ncols, chans), BF16),
            pltpu.VMEM((rows * ncols, chans), F32),
            pltpu.VMEM((chans, size.hidden), BF16),
            pltpu.VMEM((size.hidden, chans), BF16),
            pltpu.VMEM((4, *cells), BF16),
            pltpu.SemaphoreType.DMA((7 + size.pieces,)),
            pltpu.SemaphoreType.DMA((6,)),
        ],
        input_output_aliases={10 + i: i for i in range(held)},
        name="stage",
    )

    def step(stage, state):
        *state, code = state
        blocks = exchange(state[0], code & 15, ncols)
        return (
            *stage_call(
                stage.reshape(1),
                spacing_per_tier,
                columns_first(outcome_cotangent_vector[0]),
                *blocks,
                mixer_entry_projection,
                mixer_exit_projection,
                spatial_window_coefficients,
                *state,
            ),
            code >> 4,
        )

    state = lax.fori_loop(0, 2 * LAYERS, step, (*state, code))
    share = total_over_all(size, state[7])
    member_count = size.members * stochastic_displacement.shape[0]
    scale = 1.0 / math.sqrt(member_count * rows * ncols * lax.axis_size(LON))
    return (state[8][None], state[9][None], share * scale)


def solution(mesh):
    fine = Mesh(mesh.devices.reshape(-1, 2, 2, mesh.shape["mem"]), LON + ("mem",))
    placed = (
        P(None, LON, None),
        P("mem", None, LON, None),
        P("mem", None, LON, None),
        P(),
        P(),
        P(),
        P(),
    )
    return jax.shard_map(
        per_device,
        mesh=fine,
        in_specs=placed,
        out_specs=(P("mem", None, LON, None), P("mem", None, LON, None), P(None, "mem", None)),
        check_vma=False,
    )
```

```python
import functools
import math

import jax
import jax.numpy as jnp
from jax import lax
from jax.experimental import pallas as pl
from jax.experimental.pallas import tpu as pltpu
from jax.sharding import Mesh
from jax.sharding import PartitionSpec as P

MAXD = 144
LAYERS = 3
PLANE = ("xl", "core")
LON = ("z",) + PLANE
F32 = jnp.float32
BF16 = jnp.bfloat16


def passed_along(block, axis, distance):
    devices = range(lax.axis_size(axis))
    route = [((i - distance) % len(devices), i) for i in devices]
    return lax.ppermute(block, axis, route)


def slope(values):
    sig = jax.nn.sigmoid(values)
    return sig * (1.0 + values * (1.0 - sig))


def matmul(a, b, dims=((1,), (0,))):
    return lax.dot_general(a, b, (dims, ((), ())), preferred_element_type=F32)


def exchange(field, near, ncols):
    hops = (MAXD + ncols - 1) // ncols

    def within(near):
        def fetch(field):
            return (
                passed_along(field, LON, near + 1),
                passed_along(field, LON, near) if near else field,
                passed_along(field, LON, -near) if near else field,
                passed_along(field, LON, -near - 1),
            )

        return fetch

    return lax.switch(near, [within(k) for k in range(hops)], field)


class Sizes:
    def __init__(self, rows, ncols, chans, hidden):
        self.rows, self.ncols, self.chans, self.hidden = rows, ncols, chans, hidden
        self.pitch = (ncols + 15) // 16 * 16
        self.cells = rows * self.pitch


def fill_shifted(size, rest, parts, scratches):
    far_lower, near_lower, own, near_upper, far_upper = parts
    pitch, ncols = size.pitch, size.ncols
    shape = (pitch, 2 * pitch)
    col = lax.broadcasted_iota(jnp.int32, shape, 0)
    src = lax.broadcasted_iota(jnp.int32, shape, 1)
    live = (col < ncols) & (src < 2 * pitch)
    at = jnp.where(src < pitch, src, src - pitch + ncols)
    live = live & ((src < ncols) | ((src >= pitch) & (src < pitch + ncols)))
    picks = []
    for begin in (ncols - rest, rest):
        picks.append(jnp.where(live & (at == col + begin), 1.0, 0.0).astype(BF16))
    zero = jnp.zeros((pitch, size.chans), BF16)
    for scratch in scratches:
        scratch[pl.ds(0, pitch), :] = zero
        scratch[pl.ds(pitch + size.cells, pitch), :] = zero
    scratches[1][pl.ds(pitch, size.cells), :] = own
    for pick, first, second, scratch in (
        (picks[0], far_lower, near_lower, scratches[0]),
        (picks[1], near_upper, far_upper, scratches[2]),
    ):
        for row in range(size.rows):
            span = pl.ds(row * pitch, pitch)
            pair = jnp.concatenate([first[span, :], second[span, :]], axis=0)
            scratch[pl.ds(pitch + row * pitch, pitch), :] = matmul(pick, pair).astype(BF16)


def taps_of(size, scratches):
    pieces = []
    for off in range(3):
        for scratch in scratches:
            pieces.append(scratch[pl.ds(off * size.pitch, size.cells), :])
    return jnp.concatenate(pieces, axis=1)


def valid_cells(size):
    col = lax.broadcasted_iota(jnp.int32, (size.rows, size.pitch, 1), 1)
    return (col < size.ncols).reshape(size.cells, 1)


def padded_into(size, scratch, values):
    scratch[...] = jnp.zeros(scratch.shape, scratch.dtype)
    for row in range(size.rows):
        scratch[pl.ds(row * size.pitch, size.ncols), :] = values(row).astype(scratch.dtype)


def unpadded_into(size, out, values):
    for row in range(size.rows):
        out[row] = values[row * size.pitch : row * size.pitch + size.ncols, :].astype(out.dtype)


def silu(values):
    return values * jax.nn.sigmoid(values)


def turned_into(size, scratch, out, values):
    scratch[...] = values.astype(F32).reshape(size.ncols * size.rows, size.chans)
    for row in range(size.rows):
        at = row * size.pitch
        out[pl.ds(at, size.ncols), :] = scratch[pl.ds(row, size.ncols, stride=size.rows), :].astype(
            out.dtype
        )


def terms_pieces(size, layer):
    count = 9 * size.chans // size.members
    pieces = []
    for member in range(size.members):
        row = layer * count
        while row < (layer + 1) * count:
            half = row // size.each
            end = min((half + 1) * size.each, (layer + 1) * count)
            to = (half * size.members + member) * size.each
            pieces.append((member * count + row - layer * count, to + row % size.each, end - row))
            row = end
    return pieces


def begin_body(size, a_ref, b_ref, *refs):
    field, scratch = refs[0], refs[-1]
    field[...] = jnp.zeros(field.shape, field.dtype)
    turned_into(size, scratch, field, a_ref[...].astype(F32) + b_ref[...].astype(F32))


def stage_body(
    size, stage_ref, packed_ref, cot, fl, nl, nu, fu, entries, leaves, conv, field_in, grad_in, *refs
):
    field, grad_out, hidden, mixed, pre_conv, lower, upper, terms, outcome, first = refs[8:18]
    left, middle, right, back, kernel, own, narrow, pre, before, after, found, block = refs[18:30]
    wide, cot_in, leave, came_in, sems, more = refs[30:]
    stage = stage_ref[0]
    forward = stage < LAYERS
    turn = stage == LAYERS - 1
    final = stage == 2 * LAYERS - 1
    layer = jnp.where(forward, stage, 2 * LAYERS - 1 - stage)
    at = jnp.where(forward, stage, jnp.maximum(2 * LAYERS - 2 - stage, 0))
    inner = pl.ds(size.pitch, size.cells)
    blocks = [
        pltpu.make_async_copy(there, came_in.at[i], more.at[i])
        for i, there in enumerate((fl, nl, nu, fu))
    ]
    weights = [
        pltpu.make_async_copy(conv.at[layer], kernel, sems.at[0]),
        pltpu.make_async_copy(leaves.at[at], leave, more.at[5]),
    ]
    kept = (hidden, mixed, pre_conv, lower, upper)
    loads = [
        pltpu.make_async_copy(there.at[at], here, sems.at[1 + i])
        for i, (there, here) in enumerate(zip(kept, (own.at[inner], narrow, pre, before, after)))
    ]
    saves = [
        pltpu.make_async_copy(here, there.at[at], sems.at[1 + i])
        for i, (there, here) in enumerate(zip(kept, (middle.at[inner], narrow, pre, left, right)))
    ]
    for copy in blocks + weights:
        copy.start()

    fetch = pltpu.make_async_copy(cot, cot_in, more.at[4])

    @pl.when(~forward & ~final)
    def _():
        for copy in loads:
            copy.start()

    @pl.when(turn)
    def _():
        fetch.start()

    spacing = (packed_ref[0] >> (8 * layer)) & 255
    near = sum((spacing > hop * size.ncols).astype(jnp.int32) for hop in range(1, size.hops))
    shifted = (left, middle, right)
    for copy in blocks:
        copy.wait()
    parts = (came_in.at[0], came_in.at[1], field_in[...], came_in.at[2], came_in.at[3])
    fill_shifted(size, spacing - near * size.ncols, parts, shifted)
    for copy in weights:
        copy.wait()

    @pl.when(forward)
    def _():
        for copy in (saves[0], saves[3], saves[4]):
            copy.start()
        mine = middle[inner, :]
        taps = taps_of(size, shifted)
        value = matmul(taps, kernel[...])
        total = mine.astype(F32) + silu(value)
        small = total.astype(BF16)
        pre[...] = value
        narrow[...] = small
        saves[1].start()
        saves[2].start()
        act = silu(matmul(small, entries[at])).astype(BF16)
        total = total + matmul(act, leave[...])

        @pl.when(~turn)
        def _():
            field[...] = jnp.where(valid_cells(size), total, 0.0).astype(BF16)

        @pl.when(turn)
        def _():
            unpadded_into(size, block, total)
            copy = pltpu.make_async_copy(block, outcome, sems.at[6])
            copy.start()
            back[...] = jnp.zeros(back.shape, back.dtype)
            fetch.wait()
            turned_into(size, wide, back, cot_in[...])
            before[...] = left[...]
            after[...] = right[...]
            own[...] = middle[...]
            copy.wait()

        for copy in saves:
            copy.wait()

    @pl.when(~forward)
    def _():
        chans = size.chans
        turned = jnp.concatenate(
            [kernel[pl.ds((8 - tap) * chans, chans), :] for tap in range(9)], axis=1
        )
        total = grad_in[...] + matmul(taps_of(size, shifted), turned, ((1,), (1,)))
        back[...] = jnp.where(valid_cells(size), total, 0.0).astype(BF16)

        @pl.when(final)
        def _():
            unpadded_into(size, block, back)
            copy = pltpu.make_async_copy(block, first, sems.at[6])
            copy.start()
            copy.wait()

        @pl.when(~final)
        def _():
            own[pl.ds(0, size.pitch), :] = jnp.zeros((size.pitch, chans), BF16)
            own[pl.ds(size.pitch + size.cells, size.pitch), :] = jnp.zeros(
                (size.pitch, chans), BF16
            )
            for copy in loads:
                copy.wait()

    @pl.when((stage >= LAYERS - 1) & ~final)
    def _():
        came = back[...]
        pre_mlp = matmul(narrow[...], entries[at])
        grad_pre = (matmul(came, leave[...], ((1,), (1,))) * slope(pre_mlp)).astype(BF16)
        grad = came.astype(F32) + matmul(grad_pre, entries[at], ((1,), (1,)))
        grad_out[...] = grad
        grad_conv = (grad * slope(pre[...])).astype(BF16)
        field[...] = grad_conv
        taps = taps_of(size, (before, own, after))
        values = matmul(grad_conv, taps, ((0,), (0,)))
        chans = size.chans
        for tap in range(9):
            found[pl.ds(tap * chans, chans), :] = values[:, tap * chans : (tap + 1) * chans].T.astype(
                BF16
            )
        for index in range(LAYERS):

            @pl.when(at == index)
            def _(index=index):
                copies = []
                for begin, to, count in terms_pieces(size, index):
                    copies.append(
                        pltpu.make_async_copy(
                            found.at[pl.ds(begin, count)],
                            terms.at[pl.ds(to, count)],
                            sems.at[7 + len(copies)],
                        )
                    )
                for copy in copies:
                    copy.start()
                for copy in copies:
                    copy.wait()


VMEM_SPEC = pl.BlockSpec(memory_space=pltpu.VMEM)
SMEM_SPEC = pl.BlockSpec(memory_space=pltpu.SMEM)
ANY_SPEC = pl.BlockSpec(memory_space=pl.ANY)
HBM_SPEC = pl.BlockSpec(memory_space=pltpu.HBM)


def total_over_all(size, terms):
    terms = terms.reshape(2, size.members * size.each, size.chans)
    terms = jnp.sum(lax.all_to_all(terms, "core", 0, 0).astype(F32), axis=0).astype(BF16)
    terms = terms.reshape(size.members, size.each, size.chans)
    total = jnp.sum(lax.all_to_all(terms, "mem", 0, 0).astype(F32), axis=0).astype(BF16)
    depth = lax.axis_size("z")
    swaps = [("xl", [1, 0])]
    swaps += [("z", [i ^ 1 for i in range(depth)]), ("z", [i ^ 2 for i in range(depth)])]
    swaps += [("z", [depth - 1 - i for i in range(depth)])]
    for axis, partner in swaps:
        other = lax.ppermute(total, axis, list(enumerate(partner)))
        total = (total.astype(F32) + other.astype(F32)).astype(BF16)
    full = lax.all_gather(total, "core").reshape(2 * size.each, size.chans)
    own = 9 * size.chans // size.members
    return full[: LAYERS * own].reshape(LAYERS, own, size.chans).astype(F32)


def per_device(
    assimilated_snapshot,
    stochastic_displacement,
    outcome_cotangent_vector,
    spatial_window_coefficients,
    mixer_entry_projection,
    mixer_exit_projection,
    spacing_per_tier,
):
    rows, ncols, chans = assimilated_snapshot.shape
    size = Sizes(rows, ncols, chans, mixer_entry_projection.shape[2])
    size.hops = (MAXD + ncols - 1) // ncols
    size.members = lax.axis_size("mem")
    size.each = (LAYERS * 9 * chans // size.members + 31) // 32 * 16
    size.pieces = max(len(terms_pieces(size, layer)) for layer in range(LAYERS))
    tall = (size.cells + 2 * size.pitch, chans)
    cells = (size.cells, chans)

    def columns_first(values):
        return jnp.swapaxes(values, 0, 1)

    def array(*shape, dtype=BF16):
        return jax.ShapeDtypeStruct(shape, dtype)

    kinds = [
        array(*cells),
        array(*cells, dtype=F32),
        array(LAYERS, *cells),
        array(LAYERS, *cells),
        array(LAYERS, *cells, dtype=F32),
        array(LAYERS, *tall),
        array(LAYERS, *tall),
        array(2 * size.members * size.each, chans),
        array(rows, ncols, chans),
        array(rows, ncols, chans),
    ]
    held = len(kinds)
    state = pl.pallas_call(
        functools.partial(begin_body, size),
        out_shape=kinds[:2] + [pltpu.HBM(k.shape, k.dtype) for k in kinds[2:7]] + kinds[7:],
        in_specs=[VMEM_SPEC] * 2,
        out_specs=[VMEM_SPEC, ANY_SPEC] + [HBM_SPEC] * 5 + [ANY_SPEC] * 3,
        scratch_shapes=[pltpu.VMEM((rows * ncols, chans), F32)],
        name="begin",
    )(columns_first(assimilated_snapshot), columns_first(stochastic_displacement[0]))
    near = sum((spacing_per_tier > hop * ncols).astype(jnp.int32) for hop in range(1, size.hops))
    order = jnp.arange(LAYERS)
    code = jnp.sum(near * ((1 << (4 * order)) + (1 << (4 * (2 * LAYERS - 1 - order)))))
    packed = jnp.sum(spacing_per_tier << (8 * order))
    code, packed = lax.optimization_barrier((code, packed))
    code, packed = code + (1 << 28), packed + (1 << 28)
    state_specs = [VMEM_SPEC] * 2 + [HBM_SPEC] * 5 + [ANY_SPEC] * 3
    stage_call = pl.pallas_call(
        functools.partial(stage_body, size),
        out_shape=kinds[:2] + [pltpu.HBM(k.shape, k.dtype) for k in kinds[2:7]] + kinds[7:],
        in_specs=[SMEM_SPEC] * 2 + [ANY_SPEC] + [HBM_SPEC] * 4 + [VMEM_SPEC] + [HBM_SPEC] * 2 + state_specs,
        out_specs=state_specs,
        scratch_shapes=[pltpu.VMEM(tall, BF16)] * 3
        + [
            pltpu.VMEM(cells, BF16),
            pltpu.VMEM((9 * chans, chans), BF16),
            pltpu.VMEM(tall, BF16),
            pltpu.VMEM(cells, BF16),
            pltpu.VMEM(cells, F32),
            pltpu.VMEM(tall, BF16),
            pltpu.VMEM(tall, BF16),
            pltpu.VMEM((9 * chans, chans), BF16),
            pltpu.VMEM((rows, ncols, chans), BF16),
            pltpu.VMEM((rows * ncols, chans), F32),
            pltpu.VMEM((ncols, rows, chans), BF16),
            pltpu.VMEM((size.hidden, chans), BF16),
            pltpu.VMEM((4, *cells), BF16),
            pltpu.SemaphoreType.DMA((7 + size.pieces,)),
            pltpu.SemaphoreType.DMA((6,)),
        ],
        input_output_aliases={10 + i: i for i in range(held)},
        name="stage",
    )

    def step(stage, state):
        *state, code = state
        blocks = exchange(state[0], code & 15, ncols)
        return (
            *stage_call(
                stage.reshape(1),
                packed.reshape(1),
                columns_first(outcome_cotangent_vector[0]),
                *blocks,
                mixer_entry_projection,
                mixer_exit_projection,
                spatial_window_coefficients,
                *state,
            ),
            code >> 4,
        )

    state = lax.fori_loop(0, 2 * LAYERS, step, (*state, code))
    share = total_over_all(size, state[7])
    member_count = size.members * stochastic_displacement.shape[0]
    scale = 1.0 / math.sqrt(member_count * rows * ncols * lax.axis_size(LON))
    return (state[8][None], state[9][None], share * scale)


def solution(mesh):
    fine = Mesh(mesh.devices.reshape(-1, 2, 2, mesh.shape["mem"]), LON + ("mem",))
    placed = (
        P(None, LON, None),
        P("mem", None, LON, None),
        P("mem", None, LON, None),
        P(),
        P(),
        P(),
        P(),
    )
    return jax.shard_map(
        per_device,
        mesh=fine,
        in_specs=placed,
        out_specs=(P("mem", None, LON, None), P("mem", None, LON, None), P(None, "mem", None)),
        check_vma=False,
    )
```

```python
import functools
import math

import jax
import jax.numpy as jnp
from jax import lax
from jax.experimental import pallas as pl
from jax.experimental.pallas import tpu as pltpu
from jax.sharding import Mesh
from jax.sharding import PartitionSpec as P

MAXD = 144
LAYERS = 3
PLANE = ("xl", "core")
LON = ("z",) + PLANE
F32 = jnp.float32
BF16 = jnp.bfloat16


def passed_along(block, axis, distance):
    devices = range(lax.axis_size(axis))
    route = [((i - distance) % len(devices), i) for i in devices]
    return lax.ppermute(block, axis, route)


def slope(values):
    sig = jax.nn.sigmoid(values)
    return sig * (1.0 + values * (1.0 - sig))


def matmul(a, b, dims=((1,), (0,))):
    return lax.dot_general(a, b, (dims, ((), ())), preferred_element_type=F32)


def exchange(field, near, ncols):
    hops = (MAXD + ncols - 1) // ncols

    def within(near):
        def fetch(field):
            far_lower = passed_along(field, LON, near + 1)
            far_upper = passed_along(field, LON, -near - 1)
            near_lower = passed_along(field, LON, near) if near else field
            near_upper = passed_along(field, LON, -near) if near else field
            return far_lower, far_upper, near_lower, near_upper

        return fetch

    return lax.switch(near, [within(k) for k in range(hops)], field)


class Sizes:
    def __init__(self, rows, ncols, chans, hidden):
        self.rows, self.ncols, self.chans, self.hidden = rows, ncols, chans, hidden
        self.pitch = (ncols + 15) // 16 * 16
        self.cells = rows * self.pitch


def fill_shifted(size, rest, parts, scratches):
    far_lower, near_lower, own, near_upper, far_upper = parts
    pitch, ncols = size.pitch, size.ncols
    shape = (pitch, 2 * pitch)
    col = lax.broadcasted_iota(jnp.int32, shape, 0)
    src = lax.broadcasted_iota(jnp.int32, shape, 1)
    live = (col < ncols) & (src < 2 * pitch)
    at = jnp.where(src < pitch, src, src - pitch + ncols)
    live = live & ((src < ncols) | ((src >= pitch) & (src < pitch + ncols)))
    picks = []
    for begin in (ncols - rest, rest):
        picks.append(jnp.where(live & (at == col + begin), 1.0, 0.0).astype(BF16))
    zero = jnp.zeros((pitch, size.chans), BF16)
    for scratch in scratches:
        scratch[pl.ds(0, pitch), :] = zero
        scratch[pl.ds(pitch + size.cells, pitch), :] = zero
    scratches[1][pl.ds(pitch, size.cells), :] = own
    for pick, first, second, scratch in (
        (picks[0], far_lower, near_lower, scratches[0]),
        (picks[1], near_upper, far_upper, scratches[2]),
    ):
        for row in range(size.rows):
            span = pl.ds(row * pitch, pitch)
            pair = jnp.concatenate([first[span, :], second[span, :]], axis=0)
            scratch[pl.ds(pitch + row * pitch, pitch), :] = matmul(pick, pair).astype(BF16)


def taps_of(size, scratches):
    pieces = []
    for off in range(3):
        for scratch in scratches:
            pieces.append(scratch[pl.ds(off * size.pitch, size.cells), :])
    return jnp.concatenate(pieces, axis=1)


def valid_cells(size):
    col = lax.broadcasted_iota(jnp.int32, (size.rows, size.pitch, 1), 1)
    return (col < size.ncols).reshape(size.cells, 1)


def padded_into(size, scratch, values):
    scratch[...] = jnp.zeros(scratch.shape, scratch.dtype)
    for row in range(size.rows):
        scratch[pl.ds(row * size.pitch, size.ncols), :] = values(row).astype(scratch.dtype)


def unpadded_into(size, out, values):
    for row in range(size.rows):
        out[row] = values[row * size.pitch : row * size.pitch + size.ncols, :].astype(out.dtype)


def silu(values):
    return values * jax.nn.sigmoid(values)


def turned_into(size, scratch, out, values):
    scratch[...] = values.astype(F32).reshape(size.ncols * size.rows, size.chans)
    for row in range(size.rows):
        at = row * size.pitch
        out[pl.ds(at, size.ncols), :] = scratch[pl.ds(row, size.ncols, stride=size.rows), :].astype(
            out.dtype
        )


def terms_pieces(size, layer):
    count = 9 * size.chans // size.members
    pieces = []
    for member in range(size.members):
        row = layer * count
        while row < (layer + 1) * count:
            half = row // size.each
            end = min((half + 1) * size.each, (layer + 1) * count)
            to = (half * size.members + member) * size.each
            pieces.append((member * count + row - layer * count, to + row % size.each, end - row))
            row = end
    return pieces


def begin_body(size, a_ref, b_ref, *refs):
    field, scratch = refs[0], refs[-1]
    field[...] = jnp.zeros(field.shape, field.dtype)
    turned_into(size, scratch, field, a_ref[...].astype(F32) + b_ref[...].astype(F32))


def stage_body(
    size, stage_ref, packed_ref, cot, fl, nl, nu, fu, entries, leaves, conv, field_in, grad_in, *refs
):
    field, grad_out, hidden, mixed, pre_conv, lower, upper, terms, outcome, first = refs[8:18]
    left, middle, right, back, kernel, own, narrow, pre, before, after, found, block = refs[18:30]
    wide, cot_in, leave, came_in, sems, more = refs[30:]
    stage = stage_ref[0]
    forward = stage < LAYERS
    turn = stage == LAYERS - 1
    final = stage == 2 * LAYERS - 1
    layer = jnp.where(forward, stage, 2 * LAYERS - 1 - stage)
    at = jnp.where(forward, stage, jnp.maximum(2 * LAYERS - 2 - stage, 0))
    inner = pl.ds(size.pitch, size.cells)
    blocks = [
        pltpu.make_async_copy(there, came_in.at[i], more.at[i])
        for i, there in enumerate((fl, nl, nu, fu))
    ]
    weights = [
        pltpu.make_async_copy(conv.at[layer], kernel, sems.at[0]),
        pltpu.make_async_copy(leaves.at[at], leave, more.at[5]),
    ]
    kept = (hidden, mixed, pre_conv, lower, upper)
    loads = [
        pltpu.make_async_copy(there.at[at], here, sems.at[1 + i])
        for i, (there, here) in enumerate(zip(kept, (own.at[inner], narrow, pre, before, after)))
    ]
    saves = [
        pltpu.make_async_copy(here, there.at[at], sems.at[1 + i])
        for i, (there, here) in enumerate(zip(kept, (middle.at[inner], narrow, pre, left, right)))
    ]
    for copy in blocks + weights:
        copy.start()

    fetch = pltpu.make_async_copy(cot, cot_in, more.at[4])

    @pl.when(~forward & ~final)
    def _():
        for copy in loads:
            copy.start()

    @pl.when(turn)
    def _():
        fetch.start()

    spacing = (packed_ref[0] >> (8 * layer)) & 255
    near = sum((spacing > hop * size.ncols).astype(jnp.int32) for hop in range(1, size.hops))
    shifted = (left, middle, right)
    for copy in blocks:
        copy.wait()
    parts = (came_in.at[0], came_in.at[1], field_in[...], came_in.at[2], came_in.at[3])
    fill_shifted(size, spacing - near * size.ncols, parts, shifted)
    for copy in weights:
        copy.wait()

    @pl.when(forward)
    def _():
        for copy in (saves[0], saves[3], saves[4]):
            copy.start()
        mine = middle[inner, :]
        taps = taps_of(size, shifted)
        value = matmul(taps, kernel[...])
        total = mine.astype(F32) + silu(value)
        small = total.astype(BF16)
        pre[...] = value
        narrow[...] = small
        saves[1].start()
        saves[2].start()
        act = silu(matmul(small, entries[at])).astype(BF16)
        total = total + matmul(act, leave[...])

        @pl.when(~turn)
        def _():
            field[...] = jnp.where(valid_cells(size), total, 0.0).astype(BF16)

        @pl.when(turn)
        def _():
            unpadded_into(size, block, total)
            copy = pltpu.make_async_copy(block, outcome, sems.at[6])
            copy.start()
            back[...] = jnp.zeros(back.shape, back.dtype)
            fetch.wait()
            turned_into(size, wide, back, cot_in[...])
            before[...] = left[...]
            after[...] = right[...]
            own[...] = middle[...]
            copy.wait()

        for copy in saves:
            copy.wait()

    @pl.when(~forward)
    def _():
        chans = size.chans
        turned = jnp.concatenate(
            [kernel[pl.ds((8 - tap) * chans, chans), :] for tap in range(9)], axis=1
        )
        total = grad_in[...] + matmul(taps_of(size, shifted), turned, ((1,), (1,)))
        back[...] = jnp.where(valid_cells(size), total, 0.0).astype(BF16)

        @pl.when(final)
        def _():
            unpadded_into(size, block, back)
            copy = pltpu.make_async_copy(block, first, sems.at[6])
            copy.start()
            copy.wait()

        @pl.when(~final)
        def _():
            own[pl.ds(0, size.pitch), :] = jnp.zeros((size.pitch, chans), BF16)
            own[pl.ds(size.pitch + size.cells, size.pitch), :] = jnp.zeros(
                (size.pitch, chans), BF16
            )
            for copy in loads:
                copy.wait()

    @pl.when((stage >= LAYERS - 1) & ~final)
    def _():
        came = back[...]
        pre_mlp = matmul(narrow[...], entries[at])
        grad_pre = (matmul(came, leave[...], ((1,), (1,))) * slope(pre_mlp)).astype(BF16)
        grad = came.astype(F32) + matmul(grad_pre, entries[at], ((1,), (1,)))
        grad_out[...] = grad
        grad_conv = (grad * slope(pre[...])).astype(BF16)
        field[...] = grad_conv
        taps = taps_of(size, (before, own, after))
        values = matmul(grad_conv, taps, ((0,), (0,)))
        chans = size.chans
        for tap in range(9):
            found[pl.ds(tap * chans, chans), :] = values[:, tap * chans : (tap + 1) * chans].T.astype(
                BF16
            )
        for index in range(LAYERS):

            @pl.when(at == index)
            def _(index=index):
                copies = []
                for begin, to, count in terms_pieces(size, index):
                    copies.append(
                        pltpu.make_async_copy(
                            found.at[pl.ds(begin, count)],
                            terms.at[pl.ds(to, count)],
                            sems.at[7 + len(copies)],
                        )
                    )
                for copy in copies:
                    copy.start()
                for copy in copies:
                    copy.wait()


VMEM_SPEC = pl.BlockSpec(memory_space=pltpu.VMEM)
SMEM_SPEC = pl.BlockSpec(memory_space=pltpu.SMEM)
ANY_SPEC = pl.BlockSpec(memory_space=pl.ANY)
HBM_SPEC = pl.BlockSpec(memory_space=pltpu.HBM)


def total_over_all(size, terms):
    terms = terms.reshape(2, size.members * size.each, size.chans)
    terms = jnp.sum(lax.all_to_all(terms, "core", 0, 0).astype(F32), axis=0).astype(BF16)
    terms = terms.reshape(size.members, size.each, size.chans)
    total = jnp.sum(lax.all_to_all(terms, "mem", 0, 0).astype(F32), axis=0).astype(BF16)
    depth = lax.axis_size("z")
    swaps = [("xl", [1, 0])]
    swaps += [("z", [i ^ 1 for i in range(depth)]), ("z", [i ^ 2 for i in range(depth)])]
    swaps += [("z", [depth - 1 - i for i in range(depth)])]
    for axis, partner in swaps:
        other = lax.ppermute(total, axis, list(enumerate(partner)))
        total = (total.astype(F32) + other.astype(F32)).astype(BF16)
    full = lax.all_gather(total, "core").reshape(2 * size.each, size.chans)
    own = 9 * size.chans // size.members
    return full[: LAYERS * own].reshape(LAYERS, own, size.chans).astype(F32)


def per_device(
    assimilated_snapshot,
    stochastic_displacement,
    outcome_cotangent_vector,
    spatial_window_coefficients,
    mixer_entry_projection,
    mixer_exit_projection,
    spacing_per_tier,
):
    rows, ncols, chans = assimilated_snapshot.shape
    size = Sizes(rows, ncols, chans, mixer_entry_projection.shape[2])
    size.hops = (MAXD + ncols - 1) // ncols
    size.members = lax.axis_size("mem")
    size.each = (LAYERS * 9 * chans // size.members + 31) // 32 * 16
    size.pieces = max(len(terms_pieces(size, layer)) for layer in range(LAYERS))
    tall = (size.cells + 2 * size.pitch, chans)
    cells = (size.cells, chans)

    def columns_first(values):
        return jnp.swapaxes(values, 0, 1)

    def array(*shape, dtype=BF16):
        return jax.ShapeDtypeStruct(shape, dtype)

    kinds = [
        array(*cells),
        array(*cells, dtype=F32),
        array(LAYERS, *cells),
        array(LAYERS, *cells),
        array(LAYERS, *cells, dtype=F32),
        array(LAYERS, *tall),
        array(LAYERS, *tall),
        array(2 * size.members * size.each, chans),
        array(rows, ncols, chans),
        array(rows, ncols, chans),
    ]
    held = len(kinds)
    state = pl.pallas_call(
        functools.partial(begin_body, size),
        out_shape=kinds[:2] + [pltpu.HBM(k.shape, k.dtype) for k in kinds[2:7]] + kinds[7:],
        in_specs=[VMEM_SPEC] * 2,
        out_specs=[VMEM_SPEC, ANY_SPEC] + [HBM_SPEC] * 5 + [ANY_SPEC] * 3,
        scratch_shapes=[pltpu.VMEM((rows * ncols, chans), F32)],
        name="begin",
    )(columns_first(assimilated_snapshot), columns_first(stochastic_displacement[0]))
    near = sum((spacing_per_tier > hop * ncols).astype(jnp.int32) for hop in range(1, size.hops))
    order = jnp.arange(LAYERS)
    code = jnp.sum(near * ((1 << (4 * order)) + (1 << (4 * (2 * LAYERS - 1 - order)))))
    packed = jnp.sum(spacing_per_tier << (8 * order))
    code, packed = lax.optimization_barrier((code, packed))
    code, packed = code + (1 << 28), packed + (1 << 28)
    state_specs = [VMEM_SPEC] * 2 + [HBM_SPEC] * 5 + [ANY_SPEC] * 3
    stage_call = pl.pallas_call(
        functools.partial(stage_body, size),
        out_shape=kinds[:2] + [pltpu.HBM(k.shape, k.dtype) for k in kinds[2:7]] + kinds[7:],
        in_specs=[SMEM_SPEC] * 2 + [ANY_SPEC] + [HBM_SPEC] * 4 + [VMEM_SPEC] + [HBM_SPEC] * 2 + state_specs,
        out_specs=state_specs,
        scratch_shapes=[pltpu.VMEM(tall, BF16)] * 3
        + [
            pltpu.VMEM(cells, BF16),
            pltpu.VMEM((9 * chans, chans), BF16),
            pltpu.VMEM(tall, BF16),
            pltpu.VMEM(cells, BF16),
            pltpu.VMEM(cells, F32),
            pltpu.VMEM(tall, BF16),
            pltpu.VMEM(tall, BF16),
            pltpu.VMEM((9 * chans, chans), BF16),
            pltpu.VMEM((rows, ncols, chans), BF16),
            pltpu.VMEM((rows * ncols, chans), F32),
            pltpu.VMEM((ncols, rows, chans), BF16),
            pltpu.VMEM((size.hidden, chans), BF16),
            pltpu.VMEM((4, *cells), BF16),
            pltpu.SemaphoreType.DMA((7 + size.pieces,)),
            pltpu.SemaphoreType.DMA((6,)),
        ],
        input_output_aliases={10 + i: i for i in range(held)},
        name="stage",
    )

    def step(stage, state):
        *state, code = state
        far_lower, far_upper, near_lower, near_upper = exchange(state[0], code & 15, ncols)
        return (
            *stage_call(
                stage.reshape(1),
                packed.reshape(1),
                columns_first(outcome_cotangent_vector[0]),
                far_lower,
                near_lower,
                near_upper,
                far_upper,
                mixer_entry_projection,
                mixer_exit_projection,
                spatial_window_coefficients,
                *state,
            ),
            code >> 4,
        )

    state = lax.fori_loop(0, 2 * LAYERS, step, (*state, code))
    share = total_over_all(size, state[7])
    member_count = size.members * stochastic_displacement.shape[0]
    scale = 1.0 / math.sqrt(member_count * rows * ncols * lax.axis_size(LON))
    return (state[8][None], state[9][None], share * scale)


def solution(mesh):
    fine = Mesh(mesh.devices.reshape(-1, 2, 2, mesh.shape["mem"]), LON + ("mem",))
    placed = (
        P(None, LON, None),
        P("mem", None, LON, None),
        P("mem", None, LON, None),
        P(),
        P(),
        P(),
        P(),
    )
    return jax.shard_map(
        per_device,
        mesh=fine,
        in_specs=placed,
        out_specs=(P("mem", None, LON, None), P("mem", None, LON, None), P(None, "mem", None)),
        check_vma=False,
    )
```

```python
import functools
import math

import jax
import jax.numpy as jnp
from jax import lax
from jax.experimental import pallas as pl
from jax.experimental.pallas import tpu as pltpu
from jax.sharding import Mesh
from jax.sharding import PartitionSpec as P

MAXD = 144
LAYERS = 3
PLANE = ("xl", "core")
LON = ("z",) + PLANE
F32 = jnp.float32
BF16 = jnp.bfloat16


def passed_along(block, axis, distance):
    devices = range(lax.axis_size(axis))
    route = [((i - distance) % len(devices), i) for i in devices]
    return lax.ppermute(block, axis, route)


def slope(values):
    sig = jax.nn.sigmoid(values)
    return sig * (1.0 + values * (1.0 - sig))


def matmul(a, b, dims=((1,), (0,))):
    return lax.dot_general(a, b, (dims, ((), ())), preferred_element_type=F32)


def exchange(field, near, ncols):
    hops = (MAXD + ncols - 1) // ncols

    def within(near):
        def fetch(field):
            far_lower = passed_along(field, LON, near + 1)
            far_upper = passed_along(field, LON, -near - 1)
            near_lower = passed_along(field, LON, near) if near else field
            near_upper = passed_along(field, LON, -near) if near else field
            return far_lower, far_upper, near_lower, near_upper

        return fetch

    return lax.switch(near, [within(k) for k in range(hops)], field)


class Sizes:
    def __init__(self, rows, ncols, chans, hidden):
        self.rows, self.ncols, self.chans, self.hidden = rows, ncols, chans, hidden
        self.pitch = (ncols + 15) // 16 * 16
        self.cells = rows * self.pitch


def fill_shifted(size, rest, parts, scratches):
    far_lower, near_lower, own, near_upper, far_upper = parts
    pitch, ncols = size.pitch, size.ncols
    shape = (pitch, 2 * pitch)
    col = lax.broadcasted_iota(jnp.int32, shape, 0)
    src = lax.broadcasted_iota(jnp.int32, shape, 1)
    live = (col < ncols) & (src < 2 * pitch)
    at = jnp.where(src < pitch, src, src - pitch + ncols)
    live = live & ((src < ncols) | ((src >= pitch) & (src < pitch + ncols)))
    picks = []
    for begin in (ncols - rest, rest):
        picks.append(jnp.where(live & (at == col + begin), 1.0, 0.0).astype(BF16))
    zero = jnp.zeros((pitch, size.chans), BF16)
    for scratch in scratches:
        scratch[pl.ds(0, pitch), :] = zero
        scratch[pl.ds(pitch + size.cells, pitch), :] = zero
    scratches[1][pl.ds(pitch, size.cells), :] = own
    for pick, first, second, scratch in (
        (picks[0], far_lower, near_lower, scratches[0]),
        (picks[1], near_upper, far_upper, scratches[2]),
    ):
        for row in range(size.rows):
            span = pl.ds(row * pitch, pitch)
            pair = jnp.concatenate([first[span, :], second[span, :]], axis=0)
            scratch[pl.ds(pitch + row * pitch, pitch), :] = matmul(pick, pair).astype(BF16)


def taps_of(size, scratches):
    pieces = []
    for off in range(3):
        for scratch in scratches:
            pieces.append(scratch[pl.ds(off * size.pitch, size.cells), :])
    return jnp.concatenate(pieces, axis=1)


def valid_cells(size):
    col = lax.broadcasted_iota(jnp.int32, (size.rows, size.pitch, 1), 1)
    return (col < size.ncols).reshape(size.cells, 1)


def padded_into(size, scratch, values):
    scratch[...] = jnp.zeros(scratch.shape, scratch.dtype)
    for row in range(size.rows):
        scratch[pl.ds(row * size.pitch, size.ncols), :] = values(row).astype(scratch.dtype)


def unpadded_into(size, out, values):
    for row in range(size.rows):
        out[row] = values[row * size.pitch : row * size.pitch + size.ncols, :].astype(out.dtype)


def silu(values):
    return values * jax.nn.sigmoid(values)


def turned_into(size, scratch, out, values):
    scratch[...] = values.astype(F32).reshape(size.ncols * size.rows, size.chans)
    for row in range(size.rows):
        at = row * size.pitch
        out[pl.ds(at, size.ncols), :] = scratch[pl.ds(row, size.ncols, stride=size.rows), :].astype(
            out.dtype
        )


def terms_pieces(size, layer):
    count = 9 * size.chans // size.members
    pieces = []
    for member in range(size.members):
        row = layer * count
        while row < (layer + 1) * count:
            half = row // size.each
            end = min((half + 1) * size.each, (layer + 1) * count)
            to = (half * size.members + member) * size.each
            pieces.append((member * count + row - layer * count, to + row % size.each, end - row))
            row = end
    return pieces


def begin_body(size, a_ref, b_ref, *refs):
    field, scratch = refs[0], refs[-1]
    field[...] = jnp.zeros(field.shape, field.dtype)
    turned_into(size, scratch, field, a_ref[...].astype(F32) + b_ref[...].astype(F32))


def stage_body(
    size, stage_ref, packed_ref, cot, fl, nl, nu, fu, entries, leaves, conv, field_in, grad_in, *refs
):
    field, grad_out, hidden, mixed, pre_conv, lower, upper, terms, outcome, first = refs[8:18]
    left, middle, right, back, kernel, found, block, wide, cot_in, leave, came_in, sems, more = refs[18:]
    stage = stage_ref[0]
    forward = stage < LAYERS
    turn = stage == LAYERS - 1
    final = stage == 2 * LAYERS - 1
    layer = jnp.where(forward, stage, 2 * LAYERS - 1 - stage)
    at = jnp.where(forward, stage, jnp.maximum(2 * LAYERS - 2 - stage, 0))
    blocks = [
        pltpu.make_async_copy(there, came_in.at[i], more.at[i])
        for i, there in enumerate((fl, nl, nu, fu))
    ]
    weights = [
        pltpu.make_async_copy(conv.at[layer], kernel, sems.at[0]),
        pltpu.make_async_copy(leaves.at[at], leave, more.at[5]),
    ]
    for copy in blocks + weights:
        copy.start()

    fetch = pltpu.make_async_copy(cot, cot_in, more.at[4])

    @pl.when(turn)
    def _():
        fetch.start()

    @pl.when(~forward)
    def _():
        taps = taps_of(size, (lower.at[layer], hidden.at[layer], upper.at[layer]))
        values = matmul(field_in[...], taps, ((0,), (0,)))
        chans = size.chans
        for tap in range(9):
            found[pl.ds(tap * chans, chans), :] = values[:, tap * chans : (tap + 1) * chans].T.astype(
                BF16
            )
        for index in range(LAYERS):

            @pl.when(layer == index)
            def _(index=index):
                for begin, to, count in terms_pieces(size, index):
                    terms[pl.ds(to, count), :] = found[pl.ds(begin, count), :]

    spacing = (packed_ref[0] >> (8 * layer)) & 255
    near = sum((spacing > hop * size.ncols).astype(jnp.int32) for hop in range(1, size.hops))
    shifted = (left, middle, right)
    for copy in blocks:
        copy.wait()
    parts = (came_in.at[0], came_in.at[1], field_in[...], came_in.at[2], came_in.at[3])
    fill_shifted(size, spacing - near * size.ncols, parts, shifted)
    for copy in weights:
        copy.wait()

    @pl.when(forward)
    def _():
        lower[at] = left[...]
        hidden[at] = middle[...]
        upper[at] = right[...]
        mine = middle[pl.ds(size.pitch, size.cells), :]
        taps = taps_of(size, shifted)
        value = matmul(taps, kernel[...])
        total = mine.astype(F32) + silu(value)
        small = total.astype(BF16)
        pre_conv[at] = value
        mixed[at] = small
        act = silu(matmul(small, entries[at])).astype(BF16)
        total = total + matmul(act, leave[...])

        @pl.when(~turn)
        def _():
            field[...] = jnp.where(valid_cells(size), total, 0.0).astype(BF16)

        @pl.when(turn)
        def _():
            unpadded_into(size, block, total)
            copy = pltpu.make_async_copy(block, outcome, sems.at[1])
            copy.start()
            back[...] = jnp.zeros(back.shape, back.dtype)
            fetch.wait()
            turned_into(size, wide, back, cot_in[...])
            copy.wait()

    @pl.when(~forward)
    def _():
        chans = size.chans
        turned = jnp.concatenate(
            [kernel[pl.ds((8 - tap) * chans, chans), :] for tap in range(9)], axis=1
        )
        total = grad_in[...] + matmul(taps_of(size, shifted), turned, ((1,), (1,)))
        back[...] = jnp.where(valid_cells(size), total, 0.0).astype(BF16)

        @pl.when(final)
        def _():
            unpadded_into(size, block, back)
            copy = pltpu.make_async_copy(block, first, sems.at[1])
            copy.start()
            copy.wait()

    @pl.when((stage >= LAYERS - 1) & ~final)
    def _():
        came = back[...]
        pre_mlp = matmul(mixed[at], entries[at])
        grad_pre = (matmul(came, leave[...], ((1,), (1,))) * slope(pre_mlp)).astype(BF16)
        grad = came.astype(F32) + matmul(grad_pre, entries[at], ((1,), (1,)))
        grad_out[...] = grad
        field[...] = (grad * slope(pre_conv[at])).astype(BF16)


VMEM_SPEC = pl.BlockSpec(memory_space=pltpu.VMEM)
SMEM_SPEC = pl.BlockSpec(memory_space=pltpu.SMEM)
ANY_SPEC = pl.BlockSpec(memory_space=pl.ANY)
HBM_SPEC = pl.BlockSpec(memory_space=pltpu.HBM)


def total_over_all(size, terms):
    terms = terms.reshape(2, size.members * size.each, size.chans)
    terms = jnp.sum(lax.all_to_all(terms, "core", 0, 0).astype(F32), axis=0).astype(BF16)
    terms = terms.reshape(size.members, size.each, size.chans)
    total = jnp.sum(lax.all_to_all(terms, "mem", 0, 0).astype(F32), axis=0).astype(BF16)
    depth = lax.axis_size("z")
    swaps = [("xl", [1, 0])]
    swaps += [("z", [i ^ 1 for i in range(depth)]), ("z", [i ^ 2 for i in range(depth)])]
    swaps += [("z", [depth - 1 - i for i in range(depth)])]
    for axis, partner in swaps:
        other = lax.ppermute(total, axis, list(enumerate(partner)))
        total = (total.astype(F32) + other.astype(F32)).astype(BF16)
    full = lax.all_gather(total, "core").reshape(2 * size.each, size.chans)
    own = 9 * size.chans // size.members
    return full[: LAYERS * own].reshape(LAYERS, own, size.chans).astype(F32)


def per_device(
    assimilated_snapshot,
    stochastic_displacement,
    outcome_cotangent_vector,
    spatial_window_coefficients,
    mixer_entry_projection,
    mixer_exit_projection,
    spacing_per_tier,
):
    rows, ncols, chans = assimilated_snapshot.shape
    size = Sizes(rows, ncols, chans, mixer_entry_projection.shape[2])
    size.hops = (MAXD + ncols - 1) // ncols
    size.members = lax.axis_size("mem")
    size.each = (LAYERS * 9 * chans // size.members + 31) // 32 * 16
    tall = (size.cells + 2 * size.pitch, chans)
    cells = (size.cells, chans)

    def columns_first(values):
        return jnp.swapaxes(values, 0, 1)

    def array(*shape, dtype=BF16):
        return jax.ShapeDtypeStruct(shape, dtype)

    kinds = [
        array(*cells),
        array(*cells, dtype=F32),
        array(LAYERS, *tall),
        array(LAYERS, *cells),
        array(LAYERS, *cells, dtype=F32),
        array(LAYERS, *tall),
        array(LAYERS, *tall),
        array(2 * size.members * size.each, chans),
        array(rows, ncols, chans),
        array(rows, ncols, chans),
    ]
    held = len(kinds)
    state = pl.pallas_call(
        functools.partial(begin_body, size),
        out_shape=[pltpu.VMEM(k.shape, k.dtype) for k in kinds[:8]] + kinds[8:],
        in_specs=[VMEM_SPEC] * 2,
        out_specs=[VMEM_SPEC] * 8 + [ANY_SPEC] * 2,
        scratch_shapes=[pltpu.VMEM((rows * ncols, chans), F32)],
        name="begin",
    )(columns_first(assimilated_snapshot), columns_first(stochastic_displacement[0]))
    near = sum((spacing_per_tier > hop * ncols).astype(jnp.int32) for hop in range(1, size.hops))
    order = jnp.arange(LAYERS)
    code = jnp.sum(near * ((1 << (4 * order)) + (1 << (4 * (2 * LAYERS - 1 - order)))))
    packed = jnp.sum(spacing_per_tier << (8 * order))
    code, packed = lax.optimization_barrier((code, packed))
    code, packed = code + (1 << 28), packed + (1 << 28)
    state_specs = [VMEM_SPEC] * 8 + [ANY_SPEC] * 2
    stage_call = pl.pallas_call(
        functools.partial(stage_body, size),
        out_shape=[pltpu.VMEM(k.shape, k.dtype) for k in kinds[:8]] + kinds[8:],
        in_specs=[SMEM_SPEC] * 2 + [ANY_SPEC] + [HBM_SPEC] * 4 + [VMEM_SPEC] + [HBM_SPEC] * 2 + state_specs,
        out_specs=state_specs,
        scratch_shapes=[pltpu.VMEM(tall, BF16)] * 3
        + [
            pltpu.VMEM(cells, BF16),
            pltpu.VMEM((9 * chans, chans), BF16),
            pltpu.VMEM((9 * chans, chans), BF16),
            pltpu.VMEM((rows, ncols, chans), BF16),
            pltpu.VMEM((rows * ncols, chans), F32),
            pltpu.VMEM((ncols, rows, chans), BF16),
            pltpu.VMEM((size.hidden, chans), BF16),
            pltpu.VMEM((4, *cells), BF16),
            pltpu.SemaphoreType.DMA((2,)),
            pltpu.SemaphoreType.DMA((6,)),
        ],
        input_output_aliases={10 + i: i for i in range(held)},
        name="stage",
    )

    def step(stage, state):
        *state, code = state
        far_lower, far_upper, near_lower, near_upper = exchange(state[0], code & 15, ncols)
        return (
            *stage_call(
                stage.reshape(1),
                packed.reshape(1),
                columns_first(outcome_cotangent_vector[0]),
                far_lower,
                near_lower,
                near_upper,
                far_upper,
                mixer_entry_projection,
                mixer_exit_projection,
                spatial_window_coefficients,
                *state,
            ),
            code >> 4,
        )

    state = lax.fori_loop(0, 2 * LAYERS, step, (*state, code))
    share = total_over_all(size, state[7])
    member_count = size.members * stochastic_displacement.shape[0]
    scale = 1.0 / math.sqrt(member_count * rows * ncols * lax.axis_size(LON))
    return (state[8][None], state[9][None], share * scale)


def solution(mesh):
    fine = Mesh(mesh.devices.reshape(-1, 2, 2, mesh.shape["mem"]), LON + ("mem",))
    placed = (
        P(None, LON, None),
        P("mem", None, LON, None),
        P("mem", None, LON, None),
        P(),
        P(),
        P(),
        P(),
    )
    return jax.shard_map(
        per_device,
        mesh=fine,
        in_specs=placed,
        out_specs=(P("mem", None, LON, None), P("mem", None, LON, None), P(None, "mem", None)),
        check_vma=False,
    )
```

```python
import functools
import math

import jax
import jax.numpy as jnp
from jax import lax
from jax.experimental import pallas as pl
from jax.experimental.pallas import tpu as pltpu
from jax.sharding import Mesh
from jax.sharding import PartitionSpec as P

MAXD = 144
LAYERS = 3
PLANE = ("xl", "core")
LON = ("z",) + PLANE
F32 = jnp.float32
BF16 = jnp.bfloat16


def passed_along(block, axis, distance):
    devices = range(lax.axis_size(axis))
    route = [((i - distance) % len(devices), i) for i in devices]
    return lax.ppermute(block, axis, route)


def slope(values):
    sig = jax.nn.sigmoid(values)
    return sig * (1.0 + values * (1.0 - sig))


def matmul(a, b, dims=((1,), (0,))):
    return lax.dot_general(a, b, (dims, ((), ())), preferred_element_type=F32)


def exchange(field, near, ncols):
    hops = (MAXD + ncols - 1) // ncols

    def within(near):
        def fetch(field):
            far_lower = passed_along(field, LON, near + 1)
            far_upper = passed_along(field, LON, -near - 1)
            near_lower = passed_along(field, LON, near) if near else field
            near_upper = passed_along(field, LON, -near) if near else field
            return far_lower, far_upper, near_lower, near_upper

        return fetch

    return lax.switch(near, [within(k) for k in range(hops)], field)


class Sizes:
    def __init__(self, rows, ncols, chans, hidden):
        self.rows, self.ncols, self.chans, self.hidden = rows, ncols, chans, hidden
        self.pitch = (ncols + 15) // 16 * 16
        self.cells = rows * self.pitch


def fill_shifted(size, rest, parts, scratches):
    far_lower, near_lower, own, near_upper, far_upper = parts
    pitch, ncols = size.pitch, size.ncols
    shape = (pitch, 2 * pitch)
    col = lax.broadcasted_iota(jnp.int32, shape, 0)
    src = lax.broadcasted_iota(jnp.int32, shape, 1)
    live = (col < ncols) & (src < 2 * pitch)
    at = jnp.where(src < pitch, src, src - pitch + ncols)
    live = live & ((src < ncols) | ((src >= pitch) & (src < pitch + ncols)))
    picks = []
    for begin in (ncols - rest, rest):
        picks.append(jnp.where(live & (at == col + begin), 1.0, 0.0).astype(BF16))
    zero = jnp.zeros((pitch, size.chans), BF16)
    for scratch in scratches:
        scratch[pl.ds(0, pitch), :] = zero
        scratch[pl.ds(pitch + size.cells, pitch), :] = zero
    scratches[1][pl.ds(pitch, size.cells), :] = own
    for pick, first, second, scratch in (
        (picks[0], far_lower, near_lower, scratches[0]),
        (picks[1], near_upper, far_upper, scratches[2]),
    ):
        for row in range(size.rows):
            span = pl.ds(row * pitch, pitch)
            pair = jnp.concatenate([first[span, :], second[span, :]], axis=0)
            scratch[pl.ds(pitch + row * pitch, pitch), :] = matmul(pick, pair).astype(BF16)


def taps_of(size, scratches):
    pieces = []
    for off in range(3):
        for scratch in scratches:
            pieces.append(scratch[pl.ds(off * size.pitch, size.cells), :])
    return jnp.concatenate(pieces, axis=1)


def valid_cells(size):
    col = lax.broadcasted_iota(jnp.int32, (size.rows, size.pitch, 1), 1)
    return (col < size.ncols).reshape(size.cells, 1)


def padded_into(size, scratch, values):
    scratch[...] = jnp.zeros(scratch.shape, scratch.dtype)
    for row in range(size.rows):
        scratch[pl.ds(row * size.pitch, size.ncols), :] = values(row).astype(scratch.dtype)


def unpadded_into(size, out, values):
    for row in range(size.rows):
        out[row] = values[row * size.pitch : row * size.pitch + size.ncols, :].astype(out.dtype)


def silu(values):
    return values * jax.nn.sigmoid(values)


def turned_into(size, scratch, out, values):
    scratch[...] = values.astype(F32).reshape(size.ncols * size.rows, size.chans)
    for row in range(size.rows):
        at = row * size.pitch
        out[pl.ds(at, size.ncols), :] = scratch[pl.ds(row, size.ncols, stride=size.rows), :].astype(
            out.dtype
        )


def terms_pieces(size, layer):
    count = 9 * size.chans // size.members
    pieces = []
    for member in range(size.members):
        row = layer * count
        while row < (layer + 1) * count:
            half = row // size.each
            end = min((half + 1) * size.each, (layer + 1) * count)
            to = member * size.each + row % size.each
            pieces.append((member * count + row - layer * count, half, to, end - row))
            row = end
    return pieces


def begin_body(size, a_ref, b_ref, *refs):
    field, scratch = refs[0], refs[-1]
    field[...] = jnp.zeros(field.shape, field.dtype)
    turned_into(size, scratch, field, a_ref[...].astype(F32) + b_ref[...].astype(F32))


def stage_body(
    size, stage_ref, packed_ref, cot, fl, nl, nu, fu, entries, leaves, conv, field_in, grad_in, *refs
):
    field, grad_out, hidden, mixed, pre_conv, lower, upper, kept, given, outcome, first = refs[9:20]
    left, middle, right, back, kernel, own, narrow, pre, before, after, found, block = refs[20:32]
    wide, cot_in, leave, came_in, sems, more = refs[32:]
    stage = stage_ref[0]
    forward = stage < LAYERS
    turn = stage == LAYERS - 1
    final = stage == 2 * LAYERS - 1
    layer = jnp.where(forward, stage, 2 * LAYERS - 1 - stage)
    at = jnp.where(forward, stage, jnp.maximum(2 * LAYERS - 2 - stage, 0))
    inner = pl.ds(size.pitch, size.cells)
    blocks = [
        pltpu.make_async_copy(there, came_in.at[i], more.at[i])
        for i, there in enumerate((fl, nl, nu, fu))
    ]
    weights = [
        pltpu.make_async_copy(conv.at[layer], kernel, sems.at[0]),
        pltpu.make_async_copy(leaves.at[at], leave, more.at[5]),
    ]
    saved = (hidden, mixed, pre_conv, lower, upper)
    loads = [
        pltpu.make_async_copy(there.at[at], here, sems.at[1 + i])
        for i, (there, here) in enumerate(zip(saved, (own.at[inner], narrow, pre, before, after)))
    ]
    saves = [
        pltpu.make_async_copy(here, there.at[at], sems.at[1 + i])
        for i, (there, here) in enumerate(zip(saved, (middle.at[inner], narrow, pre, left, right)))
    ]
    for copy in blocks + weights:
        copy.start()

    fetch = pltpu.make_async_copy(cot, cot_in, more.at[4])

    @pl.when(~forward & ~final)
    def _():
        for copy in loads:
            copy.start()

    @pl.when(turn)
    def _():
        fetch.start()

    spacing = (packed_ref[0] >> (8 * layer)) & 255
    near = sum((spacing > hop * size.ncols).astype(jnp.int32) for hop in range(1, size.hops))
    shifted = (left, middle, right)
    for copy in blocks:
        copy.wait()
    parts = (came_in.at[0], came_in.at[1], field_in[...], came_in.at[2], came_in.at[3])
    fill_shifted(size, spacing - near * size.ncols, parts, shifted)
    for copy in weights:
        copy.wait()

    @pl.when(forward)
    def _():
        for copy in (saves[0], saves[3], saves[4]):
            copy.start()
        mine = middle[inner, :]
        taps = taps_of(size, shifted)
        value = matmul(taps, kernel[...])
        total = mine.astype(F32) + silu(value)
        small = total.astype(BF16)
        pre[...] = value
        narrow[...] = small
        saves[1].start()
        saves[2].start()
        act = silu(matmul(small, entries[at])).astype(BF16)
        total = total + matmul(act, leave[...])

        @pl.when(~turn)
        def _():
            field[...] = jnp.where(valid_cells(size), total, 0.0).astype(BF16)

        @pl.when(turn)
        def _():
            unpadded_into(size, block, total)
            copy = pltpu.make_async_copy(block, outcome, sems.at[6])
            copy.start()
            back[...] = jnp.zeros(back.shape, back.dtype)
            fetch.wait()
            turned_into(size, wide, back, cot_in[...])
            before[...] = left[...]
            after[...] = right[...]
            own[...] = middle[...]
            copy.wait()

        for copy in saves:
            copy.wait()

    @pl.when(~forward)
    def _():
        chans = size.chans
        turned = jnp.concatenate(
            [kernel[pl.ds((8 - tap) * chans, chans), :] for tap in range(9)], axis=1
        )
        total = grad_in[...] + matmul(taps_of(size, shifted), turned, ((1,), (1,)))
        back[...] = jnp.where(valid_cells(size), total, 0.0).astype(BF16)

        @pl.when(final)
        def _():
            unpadded_into(size, block, back)
            copy = pltpu.make_async_copy(block, first, sems.at[6])
            copy.start()
            copy.wait()

        @pl.when(~final)
        def _():
            own[pl.ds(0, size.pitch), :] = jnp.zeros((size.pitch, chans), BF16)
            own[pl.ds(size.pitch + size.cells, size.pitch), :] = jnp.zeros(
                (size.pitch, chans), BF16
            )
            for copy in loads:
                copy.wait()

    @pl.when((stage >= LAYERS - 1) & ~final)
    def _():
        came = back[...]
        pre_mlp = matmul(narrow[...], entries[at])
        grad_pre = (matmul(came, leave[...], ((1,), (1,))) * slope(pre_mlp)).astype(BF16)
        grad = came.astype(F32) + matmul(grad_pre, entries[at], ((1,), (1,)))
        grad_out[...] = grad
        grad_conv = (grad * slope(pre[...])).astype(BF16)
        field[...] = grad_conv
        taps = taps_of(size, (before, own, after))
        values = matmul(grad_conv, taps, ((0,), (0,)))
        chans = size.chans
        for tap in range(9):
            found[pl.ds(tap * chans, chans), :] = values[:, tap * chans : (tap + 1) * chans].T.astype(
                BF16
            )
        core = (packed_ref[0] >> 24) & 1
        for index in range(LAYERS):
            for side in range(2):

                @pl.when((at == index) & (core == side))
                def _(index=index, side=side):
                    copies = []
                    for begin, half, to, count in terms_pieces(size, index):
                        copies.append(
                            pltpu.make_async_copy(
                                found.at[pl.ds(begin, count)],
                                (kept if half == side else given).at[pl.ds(to, count)],
                                sems.at[7 + len(copies)],
                            )
                        )
                    for copy in copies:
                        copy.start()
                    for copy in copies:
                        copy.wait()


VMEM_SPEC = pl.BlockSpec(memory_space=pltpu.VMEM)
SMEM_SPEC = pl.BlockSpec(memory_space=pltpu.SMEM)
ANY_SPEC = pl.BlockSpec(memory_space=pl.ANY)
HBM_SPEC = pl.BlockSpec(memory_space=pltpu.HBM)


def total_over_all(size, kept, given):
    came = lax.ppermute(given, "core", [(0, 1), (1, 0)])
    terms = (kept.astype(F32) + came.astype(F32)).astype(BF16)
    terms = terms.reshape(size.members, size.each, size.chans)
    total = jnp.sum(lax.all_to_all(terms, "mem", 0, 0).astype(F32), axis=0).astype(BF16)
    depth = lax.axis_size("z")
    swaps = [("xl", [1, 0])]
    swaps += [("z", [i ^ 1 for i in range(depth)]), ("z", [i ^ 2 for i in range(depth)])]
    swaps += [("z", [depth - 1 - i for i in range(depth)])]
    for axis, partner in swaps:
        other = lax.ppermute(total, axis, list(enumerate(partner)))
        total = (total.astype(F32) + other.astype(F32)).astype(BF16)
    full = lax.all_gather(total, "core").reshape(2 * size.each, size.chans)
    own = 9 * size.chans // size.members
    return full[: LAYERS * own].reshape(LAYERS, own, size.chans).astype(F32)


def per_device(
    assimilated_snapshot,
    stochastic_displacement,
    outcome_cotangent_vector,
    spatial_window_coefficients,
    mixer_entry_projection,
    mixer_exit_projection,
    spacing_per_tier,
):
    rows, ncols, chans = assimilated_snapshot.shape
    size = Sizes(rows, ncols, chans, mixer_entry_projection.shape[2])
    size.hops = (MAXD + ncols - 1) // ncols
    size.members = lax.axis_size("mem")
    size.each = (LAYERS * 9 * chans // size.members + 31) // 32 * 16
    size.pieces = max(len(terms_pieces(size, layer)) for layer in range(LAYERS))
    tall = (size.cells + 2 * size.pitch, chans)
    cells = (size.cells, chans)

    def columns_first(values):
        return jnp.swapaxes(values, 0, 1)

    def array(*shape, dtype=BF16):
        return jax.ShapeDtypeStruct(shape, dtype)

    kinds = [
        array(*cells),
        array(*cells, dtype=F32),
        array(LAYERS, *cells),
        array(LAYERS, *cells),
        array(LAYERS, *cells, dtype=F32),
        array(LAYERS, *tall),
        array(LAYERS, *tall),
        array(size.members * size.each, chans),
        array(size.members * size.each, chans),
        array(rows, ncols, chans),
        array(rows, ncols, chans),
    ]
    held = len(kinds)
    state = pl.pallas_call(
        functools.partial(begin_body, size),
        out_shape=kinds[:2] + [pltpu.HBM(k.shape, k.dtype) for k in kinds[2:7]] + kinds[7:],
        in_specs=[VMEM_SPEC] * 2,
        out_specs=[VMEM_SPEC, ANY_SPEC] + [HBM_SPEC] * 5 + [ANY_SPEC] * 4,
        scratch_shapes=[pltpu.VMEM((rows * ncols, chans), F32)],
        name="begin",
    )(columns_first(assimilated_snapshot), columns_first(stochastic_displacement[0]))
    near = sum((spacing_per_tier > hop * ncols).astype(jnp.int32) for hop in range(1, size.hops))
    order = jnp.arange(LAYERS)
    code = jnp.sum(near * ((1 << (4 * order)) + (1 << (4 * (2 * LAYERS - 1 - order)))))
    packed = jnp.sum(spacing_per_tier << (8 * order)) + (lax.axis_index("core") << 24)
    code, packed = lax.optimization_barrier((code, packed))
    code, packed = code + (1 << 28), packed + (1 << 28)
    state_specs = [VMEM_SPEC] * 2 + [HBM_SPEC] * 5 + [ANY_SPEC] * 4
    stage_call = pl.pallas_call(
        functools.partial(stage_body, size),
        out_shape=kinds[:2] + [pltpu.HBM(k.shape, k.dtype) for k in kinds[2:7]] + kinds[7:],
        in_specs=[SMEM_SPEC] * 2 + [ANY_SPEC] + [HBM_SPEC] * 4 + [VMEM_SPEC] + [HBM_SPEC] * 2 + state_specs,
        out_specs=state_specs,
        scratch_shapes=[pltpu.VMEM(tall, BF16)] * 3
        + [
            pltpu.VMEM(cells, BF16),
            pltpu.VMEM((9 * chans, chans), BF16),
            pltpu.VMEM(tall, BF16),
            pltpu.VMEM(cells, BF16),
            pltpu.VMEM(cells, F32),
            pltpu.VMEM(tall, BF16),
            pltpu.VMEM(tall, BF16),
            pltpu.VMEM((9 * chans, chans), BF16),
            pltpu.VMEM((rows, ncols, chans), BF16),
            pltpu.VMEM((rows * ncols, chans), F32),
            pltpu.VMEM((ncols, rows, chans), BF16),
            pltpu.VMEM((size.hidden, chans), BF16),
            pltpu.VMEM((4, *cells), BF16),
            pltpu.SemaphoreType.DMA((7 + size.pieces,)),
            pltpu.SemaphoreType.DMA((6,)),
        ],
        input_output_aliases={10 + i: i for i in range(held)},
        name="stage",
    )

    def step(stage, state):
        *state, code = state
        far_lower, far_upper, near_lower, near_upper = exchange(state[0], code & 15, ncols)
        return (
            *stage_call(
                stage.reshape(1),
                packed.reshape(1),
                columns_first(outcome_cotangent_vector[0]),
                far_lower,
                near_lower,
                near_upper,
                far_upper,
                mixer_entry_projection,
                mixer_exit_projection,
                spatial_window_coefficients,
                *state,
            ),
            code >> 4,
        )

    state = lax.fori_loop(0, 2 * LAYERS, step, (*state, code))
    share = total_over_all(size, state[7], state[8])
    member_count = size.members * stochastic_displacement.shape[0]
    scale = 1.0 / math.sqrt(member_count * rows * ncols * lax.axis_size(LON))
    return (state[9][None], state[10][None], share * scale)


def solution(mesh):
    fine = Mesh(mesh.devices.reshape(-1, 2, 2, mesh.shape["mem"]), LON + ("mem",))
    placed = (
        P(None, LON, None),
        P("mem", None, LON, None),
        P("mem", None, LON, None),
        P(),
        P(),
        P(),
        P(),
    )
    return jax.shard_map(
        per_device,
        mesh=fine,
        in_specs=placed,
        out_specs=(P("mem", None, LON, None), P("mem", None, LON, None), P(None, "mem", None)),
        check_vma=False,
    )
```

```python
import functools
import math

import jax
import jax.numpy as jnp
from jax import lax
from jax.experimental import pallas as pl
from jax.experimental.pallas import tpu as pltpu
from jax.sharding import Mesh
from jax.sharding import PartitionSpec as P

MAXD = 144
LAYERS = 3
PLANE = ("xl", "core")
LON = ("z",) + PLANE
F32 = jnp.float32
BF16 = jnp.bfloat16


def passed_along(block, axis, distance):
    devices = range(lax.axis_size(axis))
    route = [((i - distance) % len(devices), i) for i in devices]
    return lax.ppermute(block, axis, route)


def slope(values):
    sig = jax.nn.sigmoid(values)
    return sig * (1.0 + values * (1.0 - sig))


def matmul(a, b, dims=((1,), (0,))):
    return lax.dot_general(a, b, (dims, ((), ())), preferred_element_type=F32)


def exchange(field, near, ncols):
    hops = (MAXD + ncols - 1) // ncols

    def within(near):
        def fetch(field):
            far_lower = passed_along(field, LON, near + 1)
            far_upper = passed_along(field, LON, -near - 1)
            near_lower = passed_along(field, LON, near) if near else field
            near_upper = passed_along(field, LON, -near) if near else field
            return far_lower, far_upper, near_lower, near_upper

        return fetch

    return lax.switch(near, [within(k) for k in range(hops)], field)


class Sizes:
    def __init__(self, rows, ncols, chans, hidden):
        self.rows, self.ncols, self.chans, self.hidden = rows, ncols, chans, hidden
        self.pitch = (ncols + 15) // 16 * 16
        self.cells = rows * self.pitch


def fill_shifted(size, rest, parts, scratches):
    far_lower, near_lower, own, near_upper, far_upper = parts
    pitch, ncols = size.pitch, size.ncols
    shape = (pitch, 2 * pitch)
    col = lax.broadcasted_iota(jnp.int32, shape, 0)
    src = lax.broadcasted_iota(jnp.int32, shape, 1)
    live = (col < ncols) & (src < 2 * pitch)
    at = jnp.where(src < pitch, src, src - pitch + ncols)
    live = live & ((src < ncols) | ((src >= pitch) & (src < pitch + ncols)))
    picks = []
    for begin in (ncols - rest, rest):
        picks.append(jnp.where(live & (at == col + begin), 1.0, 0.0).astype(BF16))
    zero = jnp.zeros((pitch, size.chans), BF16)
    for scratch in scratches:
        scratch[pl.ds(0, pitch), :] = zero
        scratch[pl.ds(pitch + size.cells, pitch), :] = zero
    scratches[1][pl.ds(pitch, size.cells), :] = own
    for pick, first, second, scratch in (
        (picks[0], far_lower, near_lower, scratches[0]),
        (picks[1], near_upper, far_upper, scratches[2]),
    ):
        for row in range(size.rows):
            span = pl.ds(row * pitch, pitch)
            pair = jnp.concatenate([first[span, :], second[span, :]], axis=0)
            scratch[pl.ds(pitch + row * pitch, pitch), :] = matmul(pick, pair).astype(BF16)


def taps_of(size, scratches):
    pieces = []
    for off in range(3):
        for scratch in scratches:
            pieces.append(scratch[pl.ds(off * size.pitch, size.cells), :])
    return jnp.concatenate(pieces, axis=1)


def valid_cells(size):
    col = lax.broadcasted_iota(jnp.int32, (size.rows, size.pitch, 1), 1)
    return (col < size.ncols).reshape(size.cells, 1)


def padded_into(size, scratch, values):
    scratch[...] = jnp.zeros(scratch.shape, scratch.dtype)
    for row in range(size.rows):
        scratch[pl.ds(row * size.pitch, size.ncols), :] = values(row).astype(scratch.dtype)


def unpadded_into(size, out, values):
    for row in range(size.rows):
        out[row] = values[row * size.pitch : row * size.pitch + size.ncols, :].astype(out.dtype)


def silu(values):
    return values * jax.nn.sigmoid(values)


def turned_into(size, scratch, out, values):
    scratch[...] = values.astype(F32).reshape(size.ncols * size.rows, size.chans)
    for row in range(size.rows):
        at = row * size.pitch
        out[pl.ds(at, size.ncols), :] = scratch[pl.ds(row, size.ncols, stride=size.rows), :].astype(
            out.dtype
        )


def terms_pieces(size, layer):
    count = 9 * size.chans // size.members
    pieces = []
    for member in range(size.members):
        row = layer * count
        while row < (layer + 1) * count:
            half = row // size.each
            end = min((half + 1) * size.each, (layer + 1) * count)
            to = member * size.each + row % size.each
            pieces.append((member * count + row - layer * count, half, to, end - row))
            row = end
    return pieces


def begin_body(size, a_ref, b_ref, *refs):
    field, scratch = refs[0], refs[-1]
    field[...] = jnp.zeros(field.shape, field.dtype)
    turned_into(size, scratch, field, a_ref[...].astype(F32) + b_ref[...].astype(F32))


def stage_body(
    size, stage_ref, packed_ref, cot, fl, nl, nu, fu, entries, leaves, conv, field_in, grad_in, *refs
):
    field, grad_out, hidden, mixed, pre_conv, lower, upper, kept, given, outcome, first = refs[9:20]
    left, middle, right, back, kernel, own, narrow, pre, before, after, found, block = refs[20:32]
    wide, cot_in, leave, came_in, sems, more = refs[32:]
    stage = stage_ref[0]
    forward = stage < LAYERS
    turn = stage == LAYERS - 1
    final = stage == 2 * LAYERS - 1
    layer = jnp.where(forward, stage, 2 * LAYERS - 1 - stage)
    at = jnp.where(forward, stage, jnp.maximum(2 * LAYERS - 2 - stage, 0))
    inner = pl.ds(size.pitch, size.cells)
    blocks = [
        pltpu.make_async_copy(there, came_in.at[i], more.at[i])
        for i, there in enumerate((fl, nl, nu, fu))
    ]
    weights = [
        pltpu.make_async_copy(conv.at[layer], kernel, sems.at[0]),
        pltpu.make_async_copy(leaves.at[at], leave, more.at[5]),
    ]
    saved = (hidden, mixed, pre_conv, lower, upper)
    loads = [
        pltpu.make_async_copy(there.at[at], here, sems.at[1 + i])
        for i, (there, here) in enumerate(zip(saved, (own.at[inner], narrow, pre, before, after)))
    ]
    saves = [
        pltpu.make_async_copy(here, there.at[at], sems.at[1 + i])
        for i, (there, here) in enumerate(zip(saved, (middle.at[inner], narrow, pre, left, right)))
    ]
    for copy in blocks + weights:
        copy.start()

    fetch = pltpu.make_async_copy(cot, cot_in, more.at[4])

    @pl.when(~forward & ~final)
    def _():
        for copy in loads:
            copy.start()

    @pl.when(turn)
    def _():
        fetch.start()

    spacing = (packed_ref[0] >> (8 * layer)) & 255
    near = sum((spacing > hop * size.ncols).astype(jnp.int32) for hop in range(1, size.hops))
    shifted = (left, middle, right)
    for copy in blocks:
        copy.wait()
    parts = (came_in.at[0], came_in.at[1], field_in[...], came_in.at[2], came_in.at[3])
    fill_shifted(size, spacing - near * size.ncols, parts, shifted)
    for copy in weights:
        copy.wait()

    @pl.when(forward)
    def _():
        for copy in (saves[0], saves[3], saves[4]):
            copy.start()
        mine = middle[inner, :]
        taps = taps_of(size, shifted)
        value = matmul(taps, kernel[...])
        total = mine.astype(F32) + silu(value)
        small = total.astype(BF16)
        pre[...] = value
        narrow[...] = small
        saves[1].start()
        saves[2].start()
        act = silu(matmul(small, entries[at])).astype(BF16)
        total = total + matmul(act, leave[...])

        @pl.when(~turn)
        def _():
            field[...] = jnp.where(valid_cells(size), total, 0.0).astype(BF16)

        @pl.when(turn)
        def _():
            unpadded_into(size, block, total)
            copy = pltpu.make_async_copy(block, outcome, sems.at[6])
            copy.start()
            back[...] = jnp.zeros(back.shape, back.dtype)
            fetch.wait()
            turned_into(size, wide, back, cot_in[...])
            before[...] = left[...]
            after[...] = right[...]
            own[...] = middle[...]
            copy.wait()

        for copy in saves:
            copy.wait()

    @pl.when(~forward)
    def _():
        chans = size.chans
        turned = jnp.concatenate(
            [kernel[pl.ds((8 - tap) * chans, chans), :] for tap in range(9)], axis=1
        )
        total = grad_in[...] + matmul(taps_of(size, shifted), turned, ((1,), (1,)))
        back[...] = jnp.where(valid_cells(size), total, 0.0).astype(BF16)

        @pl.when(final)
        def _():
            unpadded_into(size, block, back)
            copy = pltpu.make_async_copy(block, first, sems.at[6])
            copy.start()
            copy.wait()

        @pl.when(~final)
        def _():
            own[pl.ds(0, size.pitch), :] = jnp.zeros((size.pitch, chans), BF16)
            own[pl.ds(size.pitch + size.cells, size.pitch), :] = jnp.zeros(
                (size.pitch, chans), BF16
            )
            for copy in loads:
                copy.wait()

    @pl.when((stage >= LAYERS - 1) & ~final)
    def _():
        came = back[...]
        pre_mlp = matmul(narrow[...], entries[at])
        grad_pre = (matmul(came, leave[...], ((1,), (1,))) * slope(pre_mlp)).astype(BF16)
        grad = came.astype(F32) + matmul(grad_pre, entries[at], ((1,), (1,)))
        grad_out[...] = grad
        grad_conv = (grad * slope(pre[...])).astype(BF16)
        field[...] = grad_conv
        taps = taps_of(size, (before, own, after))
        values = matmul(grad_conv, taps, ((0,), (0,)))
        chans = size.chans
        for tap in range(9):
            found[pl.ds(tap * chans, chans), :] = values[:, tap * chans : (tap + 1) * chans].T.astype(
                BF16
            )
        core = (packed_ref[0] >> 24) & 1
        for index in range(LAYERS):
            for side in range(2):

                @pl.when((at == index) & (core == side))
                def _(index=index, side=side):
                    for begin, half, to, count in terms_pieces(size, index):
                        target = kept if half == side else given
                        target[pl.ds(to, count), :] = found[pl.ds(begin, count), :]


VMEM_SPEC = pl.BlockSpec(memory_space=pltpu.VMEM)
SMEM_SPEC = pl.BlockSpec(memory_space=pltpu.SMEM)
ANY_SPEC = pl.BlockSpec(memory_space=pl.ANY)
HBM_SPEC = pl.BlockSpec(memory_space=pltpu.HBM)


def total_over_all(size, kept, given):
    came = lax.ppermute(given, "core", [(0, 1), (1, 0)])
    terms = (kept.astype(F32) + came.astype(F32)).astype(BF16)
    terms = terms.reshape(size.members, size.each, size.chans)
    total = jnp.sum(lax.all_to_all(terms, "mem", 0, 0).astype(F32), axis=0).astype(BF16)
    depth = lax.axis_size("z")
    swaps = [("xl", [1, 0])]
    swaps += [("z", [i ^ 1 for i in range(depth)]), ("z", [i ^ 2 for i in range(depth)])]
    swaps += [("z", [depth - 1 - i for i in range(depth)])]
    for axis, partner in swaps:
        other = lax.ppermute(total, axis, list(enumerate(partner)))
        total = (total.astype(F32) + other.astype(F32)).astype(BF16)
    full = lax.all_gather(total, "core").reshape(2 * size.each, size.chans)
    own = 9 * size.chans // size.members
    return full[: LAYERS * own].reshape(LAYERS, own, size.chans).astype(F32)


def per_device(
    assimilated_snapshot,
    stochastic_displacement,
    outcome_cotangent_vector,
    spatial_window_coefficients,
    mixer_entry_projection,
    mixer_exit_projection,
    spacing_per_tier,
):
    rows, ncols, chans = assimilated_snapshot.shape
    size = Sizes(rows, ncols, chans, mixer_entry_projection.shape[2])
    size.hops = (MAXD + ncols - 1) // ncols
    size.members = lax.axis_size("mem")
    size.each = (LAYERS * 9 * chans // size.members + 31) // 32 * 16
    tall = (size.cells + 2 * size.pitch, chans)
    cells = (size.cells, chans)

    def columns_first(values):
        return jnp.swapaxes(values, 0, 1)

    def array(*shape, dtype=BF16):
        return jax.ShapeDtypeStruct(shape, dtype)

    kinds = [
        array(*cells),
        array(*cells, dtype=F32),
        array(LAYERS, *cells),
        array(LAYERS, *cells),
        array(LAYERS, *cells, dtype=F32),
        array(LAYERS, *tall),
        array(LAYERS, *tall),
        array(size.members * size.each, chans),
        array(size.members * size.each, chans),
        array(rows, ncols, chans),
        array(rows, ncols, chans),
    ]
    held = len(kinds)
    state = pl.pallas_call(
        functools.partial(begin_body, size),
        out_shape=kinds[:2] + [pltpu.HBM(k.shape, k.dtype) for k in kinds[2:7]] + kinds[7:],
        in_specs=[VMEM_SPEC] * 2,
        out_specs=[VMEM_SPEC, ANY_SPEC] + [HBM_SPEC] * 5 + [VMEM_SPEC] * 2 + [ANY_SPEC] * 2,
        scratch_shapes=[pltpu.VMEM((rows * ncols, chans), F32)],
        name="begin",
    )(columns_first(assimilated_snapshot), columns_first(stochastic_displacement[0]))
    near = sum((spacing_per_tier > hop * ncols).astype(jnp.int32) for hop in range(1, size.hops))
    order = jnp.arange(LAYERS)
    code = jnp.sum(near * ((1 << (4 * order)) + (1 << (4 * (2 * LAYERS - 1 - order)))))
    packed = jnp.sum(spacing_per_tier << (8 * order)) + (lax.axis_index("core") << 24)
    code, packed = lax.optimization_barrier((code, packed))
    code, packed = code + (1 << 28), packed + (1 << 28)
    state_specs = [VMEM_SPEC] * 2 + [HBM_SPEC] * 5 + [VMEM_SPEC] * 2 + [ANY_SPEC] * 2
    stage_call = pl.pallas_call(
        functools.partial(stage_body, size),
        out_shape=kinds[:2] + [pltpu.HBM(k.shape, k.dtype) for k in kinds[2:7]] + kinds[7:],
        in_specs=[SMEM_SPEC] * 2 + [ANY_SPEC] + [HBM_SPEC] * 4 + [VMEM_SPEC] + [HBM_SPEC] * 2 + state_specs,
        out_specs=state_specs,
        scratch_shapes=[pltpu.VMEM(tall, BF16)] * 3
        + [
            pltpu.VMEM(cells, BF16),
            pltpu.VMEM((9 * chans, chans), BF16),
            pltpu.VMEM(tall, BF16),
            pltpu.VMEM(cells, BF16),
            pltpu.VMEM(cells, F32),
            pltpu.VMEM(tall, BF16),
            pltpu.VMEM(tall, BF16),
            pltpu.VMEM((9 * chans, chans), BF16),
            pltpu.VMEM((rows, ncols, chans), BF16),
            pltpu.VMEM((rows * ncols, chans), F32),
            pltpu.VMEM((ncols, rows, chans), BF16),
            pltpu.VMEM((size.hidden, chans), BF16),
            pltpu.VMEM((4, *cells), BF16),
            pltpu.SemaphoreType.DMA((7,)),
            pltpu.SemaphoreType.DMA((6,)),
        ],
        input_output_aliases={10 + i: i for i in range(held)},
        name="stage",
    )

    def step(stage, state):
        *state, code = state
        far_lower, far_upper, near_lower, near_upper = exchange(state[0], code & 15, ncols)
        return (
            *stage_call(
                stage.reshape(1),
                packed.reshape(1),
                columns_first(outcome_cotangent_vector[0]),
                far_lower,
                near_lower,
                near_upper,
                far_upper,
                mixer_entry_projection,
                mixer_exit_projection,
                spatial_window_coefficients,
                *state,
            ),
            code >> 4,
        )

    state = lax.fori_loop(0, 2 * LAYERS, step, (*state, code))
    share = total_over_all(size, state[7], state[8])
    member_count = size.members * stochastic_displacement.shape[0]
    scale = 1.0 / math.sqrt(member_count * rows * ncols * lax.axis_size(LON))
    return (state[9][None], state[10][None], share * scale)


def solution(mesh):
    fine = Mesh(mesh.devices.reshape(-1, 2, 2, mesh.shape["mem"]), LON + ("mem",))
    placed = (
        P(None, LON, None),
        P("mem", None, LON, None),
        P("mem", None, LON, None),
        P(),
        P(),
        P(),
        P(),
    )
    return jax.shard_map(
        per_device,
        mesh=fine,
        in_specs=placed,
        out_specs=(P("mem", None, LON, None), P("mem", None, LON, None), P(None, "mem", None)),
        check_vma=False,
    )
```
